32 devices in a mesh: wave: 8 (over z, x), lev: 4 (over y, core).
Axes of the slice: x: 2, y: 2, z: 4, core: 2. Of those that a mesh axis runs over, the one named last changes fastest.
Arguments:
- spectral: bfloat16 [32, 3, 2, 72, 192], P('wave', None, None, None, 'lev'), may hold values from -6 to 6
- vertical_ops: bfloat16 [3, 72, 72], replicated, may hold values from -0.75 to 0.75
- legendre: bfloat16 [32, 2, 4, 192], P('wave'), may hold values from -0.125 to 0.125
- legendre_slope: bfloat16 [32, 2, 4, 192], P('wave'), may hold values from -4.1875 to 4.1875
- sine_lat: float32 [4], replicated, may hold values from 0.05 to 0.85
- pair_map: int32 [32], replicated, may hold values from 0 to 31, each once
- lon_counts: int32 [8], replicated, may hold values from 640 to 5120, as said below
Outputs:
- tendency: float32 [72, 8, 5120], P('lev', 'wave')
The draws below stay inside these ranges and needn't reach their ends.
Inputs may be any that keep to these rules, and one draw needn't show every extreme that they name: `pair_map`: each pair number appears once. `lon_counts`: every count is a multiple of 64; row 4 + j has the count of row j; some row has 5120.
All inputs are finite; a program needn't handle non-finite values.
Results may differ from the reference program's by a relative error of at most 0.0067.
Values may be sent and summed in bfloat16 or wider, within the bound.
No kernel may reach another device: no remote copies, remote signals or barrier semaphores. Data moves between devices by JAX's collectives and lax.ppermute only.
A program may use at most 64 MiB of HBM per device.

```python
import math
import jax
import jax.numpy as jnp
from jax import lax

LEV = 72
NLON = 5120
M = 64
SLOTS = 32
KP = 192
LATN = 4


def draw_lon_counts(key, part):
    first_key, second_key = jax.random.split(jax.random.fold_in(key, 11))
    north_counts = jax.random.randint(first_key, (LATN,), NLON // 512, NLON // 64 + 1) * 64
    widest = jax.random.randint(second_key, (), 0, LATN)
    north_counts = north_counts.at[widest].set(NLON)
    return jnp.concatenate([north_counts, north_counts]).astype(jnp.int32)


def level_of(own_key, extent, pieces, least, top_value):
    factor_of, own = 1.0, jax.random.fold_in(own_key, 6)
    for dim, shards_of in pieces:
        draws = jnp.exp(jax.random.uniform(jax.random.fold_in(own, dim), (shards_of,), jnp.float32, least / len(pieces), top_value / len(pieces)))
        factor_of = factor_of * jnp.repeat(draws, extent[dim] // shards_of).reshape([-1 if axis == dim else 1 for axis in range(len(extent))])
    return factor_of


def scatter_about(key, dims, width, bound, cuts=(), held_as=jnp.bfloat16):
    drawn = jax.random.normal(key, dims, jnp.float32) * width
    if len(cuts) > 0:
        drawn = level_of(key, dims, cuts, -0.22, 0.18) * drawn
    return jnp.clip(drawn, min=-bound, max=bound).astype(held_as)


def setup_inputs(seed: int = 0) -> dict:
    arg_keys = jax.random.split(jax.random.key(seed), 8)
    spectral = scatter_about(arg_keys[0], (SLOTS, 3, 2, LEV, KP), 1.0, 6.0, ((0, 8), (4, 4)))
    vertical_ops = scatter_about(arg_keys[1], (3, LEV, LEV), LEV ** -0.5, 0.75)
    legendre = scatter_about(arg_keys[2], (SLOTS, 2, LATN, KP), (M * M // 2) ** -0.5, 0.125, ((0, 8),))
    legendre_slope = scatter_about(arg_keys[3], (SLOTS, 2, LATN, KP), 0.7, 4.1875, ((0, 8),))
    sine_lat = jnp.clip(jax.random.uniform(arg_keys[4], (LATN,), jnp.float32, 0.05, 0.85), 0.05, 0.85)
    pair_map = jax.random.permutation(arg_keys[5], SLOTS).astype(jnp.int32)
    lon_counts = draw_lon_counts(jax.random.fold_in(arg_keys[7], 71), 0)
    return dict(spectral=spectral, vertical_ops=vertical_ops, legendre=legendre, legendre_slope=legendre_slope, sine_lat=sine_lat, pair_map=pair_map, lon_counts=lon_counts)


def make_masks(pair_numbers, total_waves, full_width):
    half_width = full_width // 2
    positions = jnp.arange(full_width, dtype=jnp.int32)
    upper_half = positions >= half_width
    offset = jnp.where(upper_half, positions - half_width, positions)
    pair_col = pair_numbers[:, None]
    first_count = jnp.where(upper_half[None, :], (total_waves - pair_col) // 2, (total_waves - pair_col + 1) // 2)
    second = jnp.where(upper_half[None, :], (pair_col + 1) // 2, (pair_col + 2) // 2)
    first_mask = (offset[None, :] < first_count).astype(jnp.float32)
    second_mask = ((offset[None, :] >= first_count) & (offset[None, :] < first_count + second)).astype(jnp.float32)
    return jnp.stack([first_mask, second_mask], axis=1)


def wave_numbers(pair_numbers, total_waves):
    return jnp.stack([pair_numbers, total_waves - 1 - pair_numbers], axis=1).reshape(-1)


def angle_table(waves, offsets, lon_count):
    products = (waves[:, None] * offsets[None, :]) % lon_count
    angles = (2.0 * math.pi) * products.astype(jnp.float32) / lon_count.astype(jnp.float32)
    return jnp.cos(angles), jnp.sin(angles)


def basis_block(waves, lon_count, start_col, block_width, total_waves):
    coarse_cols = start_col + 64 * jnp.arange(block_width // 64, dtype=jnp.int32)
    fine_cols = jnp.arange(64, dtype=jnp.int32)
    coarse_cos, coarse_sin = angle_table(waves, coarse_cols, lon_count)
    fine_cos, fine_sin = angle_table(waves, fine_cols, lon_count)
    wave_count = waves.shape[0]
    cosine = (coarse_cos[:, :, None] * fine_cos[:, None, :] - coarse_sin[:, :, None] * fine_sin[:, None, :]).reshape(wave_count, block_width)
    sine_part = (coarse_sin[:, :, None] * fine_cos[:, None, :] + coarse_cos[:, :, None] * fine_sin[:, None, :]).reshape(wave_count, block_width)
    columns = start_col + jnp.arange(block_width, dtype=jnp.int32)
    inside = (columns < lon_count).astype(jnp.float32)[None, :]
    cosine = cosine * inside
    sine_part = sine_part * inside
    weight = jnp.where(waves == 0, 1.0, jnp.where(2 * waves < lon_count, 2.0, 0.0)).astype(jnp.float32)
    plain_basis = jnp.concatenate([weight[:, None] * cosine, -weight[:, None] * sine_part], axis=0)
    factor = (waves.astype(jnp.float32) * weight / total_waves)[:, None]
    turning = jnp.concatenate([-factor * sine_part, -factor * cosine], axis=0)
    return plain_basis.astype(jnp.bfloat16), turning.astype(jnp.bfloat16)


def assemble(hemisphere_parts):
    stacked = []
    for north_part, south_part in hemisphere_parts:
        joined = jnp.concatenate([north_part, south_part], axis=-1)
        reordered = jnp.transpose(joined, (2, 4, 1, 0, 3))
        stacked.append(reordered.reshape(reordered.shape[0], reordered.shape[1], reordered.shape[2], -1))
    return jnp.stack(stacked, axis=2)


def reference(spectral, vertical_ops, legendre, legendre_slope, sine_lat, pair_map, lon_counts):
    half_width = KP // 2
    vertical = jnp.einsum('fkl,sfcln->sfckn', vertical_ops.astype(jnp.float32), spectral.astype(jnp.float32)).astype(jnp.bfloat16)
    masks = make_masks(pair_map, M, KP)
    basis_table = (legendre.astype(jnp.float32) * masks[:, :, None, :]).astype(jnp.bfloat16)
    slope_table = (legendre_slope.astype(jnp.float32) * masks[:, :, None, :]).astype(jnp.bfloat16)
    vert_wide = vertical.astype(jnp.float32)
    basis_wide = basis_table.astype(jnp.float32)
    slope_wide = slope_table.astype(jnp.float32)
    even_part = jnp.einsum('sfcln,swjn->sfclwj', vert_wide[..., :half_width], basis_wide[..., :half_width])
    odd_part = jnp.einsum('sfcln,swjn->sfclwj', vert_wide[..., half_width:], basis_wide[..., half_width:])
    even_slope = jnp.einsum('scln,swjn->sclwj', vert_wide[:, 2, ..., :half_width], slope_wide[..., :half_width])
    odd_slope = jnp.einsum('scln,swjn->sclwj', vert_wide[:, 2, ..., half_width:], slope_wide[..., half_width:])
    fourier = assemble([
        (even_part[:, 0] + odd_part[:, 0], even_part[:, 0] - odd_part[:, 0]),
        (even_part[:, 1] + odd_part[:, 1], even_part[:, 1] - odd_part[:, 1]),
        (even_slope + odd_slope, odd_slope - even_slope),
        (even_part[:, 2] + odd_part[:, 2], even_part[:, 2] - odd_part[:, 2]),
    ]).astype(jnp.bfloat16)
    rows_sine = jnp.concatenate([sine_lat, -sine_lat]).astype(jnp.float32)
    waves = wave_numbers(pair_map, M)

    def one_row(row_index):
        coeffs = lax.dynamic_index_in_dim(fourier, row_index, 1, keepdims=False).reshape(LEV, 4, 2 * M)
        sine_row = rows_sine[row_index]
        plain_basis, turning = basis_block(waves, lon_counts[row_index], 0, NLON, M)
        three_fields = coeffs[:, 0:3].reshape(LEV * 3, 2 * M)
        grid_values = jnp.dot(three_fields, plain_basis, preferred_element_type=jnp.float32).reshape(LEV, 3, NLON)
        zonal_slope = jnp.dot(coeffs[:, 3], turning, preferred_element_type=jnp.float32)
        return -(grid_values[:, 0] * zonal_slope / (1.0 - sine_row * sine_row) + grid_values[:, 1] * grid_values[:, 2] / M)

    output = lax.map(one_row, jnp.arange(2 * LATN, dtype=jnp.int32))
    return jnp.transpose(output, (1, 0, 2))
```

```python
import functools
import math

import jax
import jax.numpy as jnp
from jax import lax
from jax.experimental import pallas as pl
from jax.experimental.pallas import tpu as pltpu
from jax.sharding import PartitionSpec as P

NLON = 5120
FIELDS = 4
LANES = 128
COLS = 512

F32 = jnp.float32
BF16 = jnp.bfloat16
NT = (((1,), (1,)), ((), ()))
TN = (((0,), (0,)), ((), ()))


def dot(a, b, dims=(((1,), (0,)), ((), ()))):
    return lax.dot_general(a, b, dims, preferred_element_type=F32)


def iota(shape, dim):
    return lax.broadcasted_iota(jnp.int32, shape, dim)


def row_pairs(pair_ref, first, count, shape):
    slot = iota(shape, 0) // 2
    numbers = jnp.zeros(shape, jnp.int32)
    for index in range(count):
        numbers = jnp.where(slot == index, pair_ref[first + index], numbers)
    return numbers


def partial_kernel(
    sizes, pair_ref, spectral_ref, ops_ref, legendre_ref, slope_ref, send_ref, table_ref
):
    pairs, level_ranks, levels_out, pad, total_waves = sizes
    _, fields, parts, width, levels = spectral_ref.shape
    _, orders, lats, full = legendre_ref.shape
    half = full // 2
    rank = lax.axis_index("lev")
    first_pair = lax.axis_index("wave") * pairs
    sub = pairs * orders
    rows = lats * parts * sub
    cols = pairs * parts * width

    for t, ref in enumerate((legendre_ref, slope_ref)):
        for s in range(pairs):
            for w in range(orders):
                base = ((t * pairs + s) * orders + w) * lats
                table_ref[base : base + lats, :] = ref[s, w].astype(F32)
    table = table_ref[...].astype(BF16)

    r = iota((2 * rows, 2 * sub * lats), 0)
    t, j, sw = r // rows, (r % rows) // (parts * sub), r % sub
    wanted = (t * sub + sw) * lats + j
    pick = (iota(r.shape, 1) == wanted).astype(F32).astype(BF16)
    picked = dot(pick, table).astype(BF16)
    shape = (full, cols)
    place = (iota(shape, 0) == rank * width + iota(shape, 1) % width).astype(F32).astype(BF16)
    spread = dot(picked, place)

    shape = (rows, cols)
    r, col = iota(shape, 0), iota(shape, 1)
    part, slot, order = (r // sub) % parts, (r % sub) // orders, r % orders
    number = jnp.zeros(shape, jnp.int32)
    for s in range(pairs):
        number = jnp.where(slot == s, pair_ref[first_pair + s], number)
    position = rank * width + col % width
    upper = (position >= half).astype(jnp.int32)
    offset = position - half * upper
    count0 = (total_waves - number + 1 - upper) >> 1
    count1 = (number + 2 - upper) >> 1
    low = jnp.where(order == 0, 0, count0)
    high = jnp.where(order == 0, count0, count0 + count1)
    block = col // width
    keep = (offset >= low) & (offset < high) & (block == slot * parts + part)
    basis = jnp.where(keep, spread[:rows], 0.0).astype(BF16)
    slope_basis = jnp.where(keep, spread[rows:], 0.0).astype(BF16)

    shape = (level_ranks * pad, levels)
    r = iota(shape, 0)
    level = jnp.where(r % pad < levels_out, (r // pad) * levels_out + r % pad, -1)
    spread_levels = (iota(shape, 1) == level).astype(F32).astype(BF16)
    sums = []
    for f in range(fields):
        operator = dot(spread_levels, ops_ref[f]).astype(BF16)
        field = spectral_ref[:, f].reshape(cols, levels)
        vertical = dot(field, operator, NT).astype(BF16)
        sums.append(dot(basis, vertical))
        if f == 2:
            sums.insert(2, dot(slope_basis, vertical))

    south = jnp.where(rank * width < half, 1.0, -1.0)
    lane_field = iota((rows, FIELDS * pad), 1) // pad
    factor = jnp.where(lane_field == 2, -south, south)
    for d in range(level_ranks):
        joined = jnp.concatenate([x[:, d * pad : (d + 1) * pad] for x in sums], axis=1)
        mirrored = joined * factor
        for j in range(lats):
            piece = slice(j * parts * sub, (j + 1) * parts * sub)
            send_ref[j * level_ranks + d] = joined[piece].astype(BF16)
            send_ref[(lats + j) * level_ranks + d] = mirrored[piece].astype(BF16)


def modulo(values, modulus):
    quotient = jnp.floor(values / modulus)
    left = values - quotient * modulus
    left = jnp.where(left < 0, left + modulus, left)
    return jnp.where(left >= modulus, left - modulus, left)


def wave_column(pairs_ref, total_waves):
    slots = pairs_ref.shape[1]
    shape = (2 * slots, slots)
    mine = iota(shape, 1) == iota(shape, 0) // 2
    numbers = jnp.broadcast_to(pairs_ref[...], shape)
    number = jnp.sum(jnp.where(mine, numbers, 0).astype(F32), axis=1, keepdims=True)
    second = iota(number.shape, 0) % 2 == 1
    return jnp.where(second, total_waves - 1 - number, number)


def basis_kernel(total_waves, group, counts_ref, pairs_ref, basis_ref):
    count = counts_ref[lax.axis_index("wave")].astype(F32)
    waves = wave_column(pairs_ref, total_waves)
    weight = jnp.where(waves == 0, 1.0, jnp.where(2 * waves < count, 2.0, 0.0))
    tiles = NLON // LANES

    def table(step, length):
        turns = modulo(waves * (step * iota((1, length), 1)).astype(F32), count)
        angle = (2.0 * math.pi) * turns / count
        return jnp.cos(angle), jnp.sin(angle)

    coarse_cos, coarse_sin = table(LANES, LANES)
    fine_cos, fine_sin = table(1, LANES)
    coarse_cos, coarse_sin = coarse_cos * weight, coarse_sin * weight
    for t in range(tiles):
        a, b = coarse_cos[:, t : t + 1], coarse_sin[:, t : t + 1]
        cosine = (a * fine_cos - b * fine_sin).reshape(-1, 1, group, LANES)
        sine = (b * fine_cos + a * fine_sin).reshape(-1, 1, group, LANES)
        both = jnp.concatenate([cosine, -sine], axis=1).reshape(-1, LANES)
        basis_ref[:, t * LANES : (t + 1) * LANES] = both.astype(BF16)


def grid_kernel(sizes, counts_ref, sine_ref, pairs_ref, received_ref, basis_ref, out_ref):
    level_ranks, levels_out, pad, group, total_waves = sizes
    lats = sine_ref.shape[0]
    row = lax.axis_index("wave")
    count = counts_ref[row]
    sine = jnp.where(row < lats, sine_ref[lax.rem(row, lats)], -sine_ref[lax.rem(row, lats)])
    chunks, chunk_rows, lanes = received_ref.shape
    sources = chunks // level_ranks
    data = received_ref[...].astype(F32).reshape(sources, level_ranks, chunk_rows, lanes)
    total = jnp.sum(data, axis=1)

    waves = wave_column(pairs_ref, total_waves).reshape(sources, group, 1) / total_waves
    real, imag = total[:, :group], total[:, group:]
    turned = jnp.concatenate([-waves * imag, waves * real], axis=1)
    zonal_lane = iota(total.shape, 2) // pad == 3
    total = jnp.where(zonal_lane, turned, total).reshape(sources * chunk_rows, lanes)
    by_level = total.T
    keep = -(-levels_out // 8) * 8
    coeffs = jnp.concatenate([by_level[g * pad : g * pad + keep] for g in range(FIELDS)], axis=0)
    coeffs = coeffs.astype(BF16)

    inverse = 1.0 / (1.0 - jnp.full((1, 1), sine * sine))
    for start in range(0, NLON, COLS):
        values = dot(coeffs, basis_ref[:, start : start + COLS])
        first, second, third, fourth = (values[g * keep : g * keep + levels_out] for g in range(4))
        result = -(first * fourth * inverse + second * third * (1.0 / total_waves))
        inside = start + iota(result.shape, 1) < count
        out_ref[:, 0, start : start + COLS] = jnp.where(inside, result, 0.0)


def per_device(spectral, vertical_ops, legendre, legendre_slope, sine_lat, pair_map, lon_counts):
    pairs, _, parts, levels, width = spectral.shape
    level_ranks = lax.axis_size("lev")
    rows = lax.axis_size("wave")
    slots = pair_map.shape[0]
    total_waves = 2 * slots
    levels_out = levels // level_ranks
    pad = LANES // FIELDS
    lats = sine_lat.shape[0]
    orders = legendre.shape[1]
    group = pairs * orders
    assert rows == 2 * lats == lon_counts.shape[0]
    assert levels_out <= pad
    assert (width * level_ranks // 2) % width == 0

    smem = pl.BlockSpec(memory_space=pltpu.SMEM)
    vmem = pl.BlockSpec(memory_space=pltpu.VMEM)
    by_position = jnp.transpose(spectral, (0, 1, 2, 4, 3))
    pair_row = pair_map.reshape(1, slots)
    send = pl.pallas_call(
        functools.partial(partial_kernel, (pairs, level_ranks, levels_out, pad, total_waves)),
        out_shape=jax.ShapeDtypeStruct((rows * level_ranks, parts * group, FIELDS * pad), BF16),
        in_specs=[smem, vmem, vmem, vmem, vmem],
        out_specs=vmem,
        scratch_shapes=[pltpu.VMEM((2 * group * lats, legendre.shape[3]), F32)],
        name="partial_sums",
    )(pair_map, by_position, vertical_ops, legendre, legendre_slope)
    received = lax.all_to_all(send, ("wave", "lev"), split_axis=0, concat_axis=0, tiled=True)
    basis = pl.pallas_call(
        functools.partial(basis_kernel, total_waves, group),
        out_shape=jax.ShapeDtypeStruct((4 * slots, NLON), BF16),
        in_specs=[smem, vmem],
        out_specs=vmem,
        name="zonal_basis",
    )(lon_counts, pair_row)
    return pl.pallas_call(
        functools.partial(grid_kernel, (level_ranks, levels_out, pad, group, total_waves)),
        out_shape=jax.ShapeDtypeStruct((levels_out, 1, NLON), F32),
        in_specs=[smem, smem, vmem, vmem, vmem],
        out_specs=vmem,
        name="grid_tendency",
    )(lon_counts, sine_lat, pair_row, received, basis)


def solution(mesh):
    placed = (
        P("wave", None, None, None, "lev"),
        P(),
        P("wave", None, None, None),
        P("wave", None, None, None),
        P(),
        P(),
        P(),
    )
    return jax.shard_map(
        per_device, mesh=mesh, in_specs=placed, out_specs=P("lev", "wave", None), check_vma=False
    )
```

```python
import functools
import math

import jax
import jax.numpy as jnp
from jax import lax
from jax.experimental import pallas as pl
from jax.experimental.pallas import tpu as pltpu
from jax.sharding import PartitionSpec as P

NLON = 5120
FIELDS = 4
LANES = 128
COLS = 1280
RESIDENT = 4 << 20

F32 = jnp.float32
BF16 = jnp.bfloat16
NT = (((1,), (1,)), ((), ()))
TN = (((0,), (0,)), ((), ()))


def dot(a, b, dims=(((1,), (0,)), ((), ()))):
    return lax.dot_general(a, b, dims, preferred_element_type=F32)


def iota(shape, dim):
    return lax.broadcasted_iota(jnp.int32, shape, dim)


def row_pairs(pair_ref, first, count, shape):
    slot = iota(shape, 0) // 2
    numbers = jnp.zeros(shape, jnp.int32)
    for index in range(count):
        numbers = jnp.where(slot == index, pair_ref[first + index], numbers)
    return numbers


def partial_kernel(
    sizes,
    pair_hbm,
    spectral_hbm,
    ops_hbm,
    legendre_hbm,
    slope_hbm,
    send_ref,
    pair_ref,
    spectral_ref,
    ops_ref,
    legendre_ref,
    slope_ref,
    table_ref,
    arrived,
):
    pairs, level_ranks, levels_out, pad, total_waves = sizes
    _, fields, parts, width, levels = spectral_ref.shape
    _, orders, lats, full = legendre_ref.shape
    copies = [
        pltpu.make_async_copy(source, target, arrived.at[index])
        for index, (source, target) in enumerate(
            [(legendre_hbm, legendre_ref), (slope_hbm, slope_ref), (pair_hbm, pair_ref)]
            + [(ops_hbm, ops_ref)]
            + [(spectral_hbm.at[:, f], spectral_ref.at[:, f]) for f in range(fields)]
        )
    ]
    for copy in copies:
        copy.start()
    half = full // 2
    rank = lax.axis_index("lev")
    first_pair = lax.axis_index("wave") * pairs
    sub = pairs * orders
    rows = lats * parts * sub
    cols = pairs * parts * width

    r = iota((2 * rows, 2 * sub * lats), 0)
    t, j, sw = r // rows, (r % rows) // (parts * sub), r % sub
    wanted = (t * sub + sw) * lats + j
    pick = (iota(r.shape, 1) == wanted).astype(F32).astype(BF16)
    shape = (full, cols)
    place = (iota(shape, 0) == rank * width + iota(shape, 1) % width).astype(F32).astype(BF16)
    shape = (level_ranks * pad, levels)
    r = iota(shape, 0)
    level = jnp.where(r % pad < levels_out, (r // pad) * levels_out + r % pad, -1)
    spread_levels = (iota(shape, 1) == level).astype(F32).astype(BF16)

    for copy in copies[:2]:
        copy.wait()
    for t, ref in enumerate((legendre_ref, slope_ref)):
        for s in range(pairs):
            for w in range(orders):
                base = ((t * pairs + s) * orders + w) * lats
                table_ref[base : base + lats, :] = ref[s, w].astype(F32)
    table = table_ref[...].astype(BF16)

    picked = dot(pick, table).astype(BF16)
    spread = dot(picked, place)

    copies[2].wait()
    shape = (rows, cols)
    r, col = iota(shape, 0), iota(shape, 1)
    part, slot, order = (r // sub) % parts, (r % sub) // orders, r % orders
    number = jnp.zeros(shape, jnp.int32)
    for s in range(pairs):
        number = jnp.where(slot == s, pair_ref[first_pair + s], number)
    position = rank * width + col % width
    upper = (position >= half).astype(jnp.int32)
    offset = position - half * upper
    count0 = (total_waves - number + 1 - upper) >> 1
    count1 = (number + 2 - upper) >> 1
    low = jnp.where(order == 0, 0, count0)
    high = jnp.where(order == 0, count0, count0 + count1)
    block = col // width
    keep = (offset >= low) & (offset < high) & (block == slot * parts + part)
    basis = jnp.where(keep, spread[:rows], 0.0).astype(BF16)
    slope_basis = jnp.where(keep, spread[rows:], 0.0).astype(BF16)

    sums = []
    copies[3].wait()
    for f in range(fields):
        copies[4 + f].wait()
        operator = dot(spread_levels, ops_ref[f]).astype(BF16)
        field = spectral_ref[:, f].reshape(cols, levels)
        vertical = dot(field, operator, NT).astype(BF16)
        sums.append(dot(basis, vertical))
        if f == 2:
            sums.insert(2, dot(slope_basis, vertical))

    south = jnp.where(rank * width < half, 1.0, -1.0)
    lane_field = iota((rows, FIELDS * pad), 1) // pad
    factor = jnp.where(lane_field == 2, -south, south)
    for d in range(level_ranks):
        joined = jnp.concatenate([x[:, d * pad : (d + 1) * pad] for x in sums], axis=1)
        mirrored = joined * factor
        for j in range(lats):
            piece = slice(j * parts * sub, (j + 1) * parts * sub)
            send_ref[j * level_ranks + d] = joined[piece].astype(BF16)
            send_ref[(lats + j) * level_ranks + d] = mirrored[piece].astype(BF16)


def modulo(values, modulus):
    quotient = jnp.floor(values / modulus)
    left = values - quotient * modulus
    left = jnp.where(left < 0, left + modulus, left)
    return jnp.where(left >= modulus, left - modulus, left)


def wave_column(pairs_ref, total_waves):
    slots = pairs_ref.shape[1]
    shape = (2 * slots, slots)
    mine = iota(shape, 1) == iota(shape, 0) // 2
    numbers = jnp.broadcast_to(pairs_ref[...], shape)
    number = jnp.sum(jnp.where(mine, numbers, 0).astype(F32), axis=1, keepdims=True)
    second = iota(number.shape, 0) % 2 == 1
    return jnp.where(second, total_waves - 1 - number, number)


def basis_kernel(total_waves, group, counts_ref, sine_ref, pairs_ref, basis_ref, aux_ref):
    lats = sine_ref.shape[0]
    row = lax.axis_index("wave")
    count = counts_ref[row].astype(F32)
    waves = wave_column(pairs_ref, total_waves)
    wave_rows = waves.shape[0]
    sine = jnp.where(row < lats, sine_ref[lax.rem(row, lats)], -sine_ref[lax.rem(row, lats)])
    inverse = 1.0 / (1.0 - jnp.full((8, LANES), sine * sine))
    aux_ref[:wave_rows] = jnp.broadcast_to(waves / total_waves, (wave_rows, LANES))
    aux_ref[wave_rows : wave_rows + 8] = inverse
    aux_ref[wave_rows + 8 :] = jnp.full((8, LANES), count)
    weight = jnp.where(waves == 0, 1.0, jnp.where(2 * waves < count, 2.0, 0.0))
    tiles = NLON // LANES

    def table(step, length):
        turns = modulo(waves * (step * iota((1, length), 1)).astype(F32), count)
        angle = (2.0 * math.pi) * turns / count
        return jnp.cos(angle), jnp.sin(angle)

    coarse_cos, coarse_sin = table(LANES, LANES)
    fine_cos, fine_sin = table(1, LANES)
    coarse_cos, coarse_sin = coarse_cos * weight, coarse_sin * weight
    for t in range(tiles):
        a, b = coarse_cos[:, t : t + 1], coarse_sin[:, t : t + 1]
        cosine = (a * fine_cos - b * fine_sin).reshape(-1, 1, group, LANES)
        sine = (b * fine_cos + a * fine_sin).reshape(-1, 1, group, LANES)
        both = jnp.concatenate([cosine, -sine], axis=1).reshape(-1, LANES)
        basis_ref[:, t * LANES : (t + 1) * LANES] = both.astype(BF16)


def grid_kernel(sizes, received_ref, basis_ref, aux_ref, out_hbm, out_ref, sent):
    level_ranks, levels_out, pad, group, total_waves = sizes
    chunks, chunk_rows, lanes = received_ref.shape
    sources = chunks // level_ranks
    data = received_ref[...].astype(F32).reshape(sources, level_ranks, chunk_rows, lanes)
    total = jnp.sum(data, axis=1)

    wave_rows = sources * group
    waves = aux_ref[:wave_rows].reshape(sources, group, LANES)
    real, imag = total[:, :group], total[:, group:]
    turned = jnp.concatenate([-waves * imag, waves * real], axis=1)
    zonal_lane = iota(total.shape, 2) // pad == 3
    total = jnp.where(zonal_lane, turned, total).reshape(sources * chunk_rows, lanes)
    by_level = total.T
    keep = -(-levels_out // 8) * 8
    coeffs = jnp.concatenate([by_level[g * pad : g * pad + keep] for g in range(FIELDS)], axis=0)
    coeffs = coeffs.astype(BF16)

    inverse = aux_ref[wave_rows : wave_rows + 1, :1]
    count = aux_ref[wave_rows + 8 : wave_rows + 9, :1]
    copies = []
    for start in range(0, NLON, COLS):
        values = dot(coeffs, basis_ref[:, start : start + COLS])
        first, second, third, fourth = (values[g * keep : g * keep + levels_out] for g in range(4))
        result = -(first * fourth * inverse + second * third * (1.0 / total_waves))
        inside = (start + iota(result.shape, 1)).astype(F32) < count
        window = (slice(None), slice(None), slice(start, start + COLS))
        out_ref[:, 0, start : start + COLS] = jnp.where(inside, result, 0.0)
        copy = pltpu.make_async_copy(
            out_ref.at[window], out_hbm.at[window], sent.at[start // COLS]
        )
        copy.start()
        copies.append(copy)
    for copy in copies:
        copy.wait()


def per_device(spectral, vertical_ops, legendre, legendre_slope, sine_lat, pair_map, lon_counts):
    pairs, _, parts, levels, width = spectral.shape
    level_ranks = lax.axis_size("lev")
    rows = lax.axis_size("wave")
    slots = pair_map.shape[0]
    total_waves = 2 * slots
    levels_out = levels // level_ranks
    pad = LANES // FIELDS
    lats = sine_lat.shape[0]
    orders = legendre.shape[1]
    group = pairs * orders
    assert rows == 2 * lats == lon_counts.shape[0]
    assert levels_out <= pad
    assert (width * level_ranks // 2) % width == 0

    smem = pl.BlockSpec(memory_space=pltpu.SMEM)
    vmem = pl.BlockSpec(memory_space=pltpu.VMEM)
    hbm = pl.BlockSpec(memory_space=pl.ANY)
    by_position = jnp.transpose(spectral, (0, 1, 2, 4, 3))
    fields = spectral.shape[1]
    resident = 4 * slots * NLON * 2 <= RESIDENT
    placed = pltpu.VMEM if resident else jax.ShapeDtypeStruct
    send = pl.pallas_call(
        functools.partial(partial_kernel, (pairs, level_ranks, levels_out, pad, total_waves)),
        out_shape=pltpu.VMEM((rows * level_ranks, parts * group, FIELDS * pad), BF16),
        in_specs=[hbm] * 5,
        out_specs=vmem,
        scratch_shapes=[
            pltpu.SMEM(pair_map.shape, pair_map.dtype),
            pltpu.VMEM(by_position.shape, BF16),
            pltpu.VMEM(vertical_ops.shape, BF16),
            pltpu.VMEM(legendre.shape, BF16),
            pltpu.VMEM(legendre.shape, BF16),
            pltpu.VMEM((2 * group * lats, legendre.shape[3]), F32),
            pltpu.SemaphoreType.DMA((4 + fields,)),
        ],
        name="partial_sums",
    )(pair_map, by_position, vertical_ops, legendre, legendre_slope)
    received = lax.all_to_all(send, ("wave", "lev"), split_axis=0, concat_axis=0, tiled=True)
    basis, aux = pl.pallas_call(
        functools.partial(basis_kernel, total_waves, group),
        out_shape=[
            placed((4 * slots, NLON), BF16),
            pltpu.VMEM((2 * slots + 16, LANES), F32),
        ],
        in_specs=[smem, smem, vmem],
        out_specs=[vmem, vmem],
        name="zonal_basis",
    )(lon_counts, sine_lat, pair_map.reshape(1, slots))
    received, aux = (
        pltpu.with_memory_space_constraint(x, pltpu.VMEM) for x in (received, aux)
    )
    if resident:
        basis = pltpu.with_memory_space_constraint(basis, pltpu.VMEM)
    return pl.pallas_call(
        functools.partial(grid_kernel, (level_ranks, levels_out, pad, group, total_waves)),
        out_shape=jax.ShapeDtypeStruct((levels_out, 1, NLON), F32),
        in_specs=[vmem, vmem, vmem],
        out_specs=hbm,
        scratch_shapes=[
            pltpu.VMEM((levels_out, 1, NLON), F32),
            pltpu.SemaphoreType.DMA((NLON // COLS,)),
        ],
        name="grid_tendency",
    )(received, basis, aux)


def solution(mesh):
    placed = (
        P("wave", None, None, None, "lev"),
        P(),
        P("wave", None, None, None),
        P("wave", None, None, None),
        P(),
        P(),
        P(),
    )
    return jax.shard_map(
        per_device, mesh=mesh, in_specs=placed, out_specs=P("lev", "wave", None), check_vma=False
    )
```

```python
import functools
import math

import jax
import jax.numpy as jnp
from jax import lax
from jax.experimental import pallas as pl
from jax.experimental.pallas import tpu as pltpu
from jax.sharding import PartitionSpec as P

NLON = 5120
FIELDS = 4
LANES = 128
COLS = 1280
RESIDENT = 4 << 20

F32 = jnp.float32
BF16 = jnp.bfloat16
NT = (((1,), (1,)), ((), ()))


def dot(a, b, dims=(((1,), (0,)), ((), ()))):
    return lax.dot_general(a, b, dims, preferred_element_type=F32)


def iota(shape, dim):
    return lax.broadcasted_iota(jnp.int32, shape, dim)


def cos_sin(products, count, inverse):
    quarters = jnp.floor(products * 4.0 * inverse + 0.5)
    angle = (products * 4.0 - quarters * count) * inverse * (0.5 * math.pi)
    square = angle * angle
    sine = square * (1.0 / 362880.0) - 1.0 / 5040.0
    sine = square * sine + 1.0 / 120.0
    sine = square * sine - 1.0 / 6.0
    sine = angle + angle * (square * sine)
    cosine = square * (1.0 / 40320.0) - 1.0 / 720.0
    cosine = square * cosine + 1.0 / 24.0
    cosine = square * cosine - 0.5
    cosine = square * cosine + 1.0
    turn = quarters.astype(jnp.int32) & 3
    swap = (turn & 1) == 1
    first = jnp.where(swap, sine, cosine)
    second = jnp.where(swap, cosine, sine)
    first = jnp.where((turn == 1) | (turn == 2), -first, first)
    second = jnp.where(turn >= 2, -second, second)
    return first, second


def zonal_tables(sizes, count, sine, pair_ref, basis_ref, aux_ref, coarse_ref):
    pairs, orders, parts, total_waves = sizes
    lanes = basis_ref.shape[1]
    sub = pairs * orders
    shape = (8, lanes)
    lane = iota(shape, 1)
    slot = (lane // (parts * sub)) * pairs + (lane % sub) // orders
    number = jnp.zeros(shape, jnp.int32)
    for index in range(total_waves // 2):
        number = jnp.where(slot == index, pair_ref[index], number)
    waves = jnp.where(lane % orders == 1, total_waves - 1 - number, number).astype(F32)
    imag = (lane // sub) % parts == 1
    aux_ref[:8] = jnp.where(imag, waves, -waves) / total_waves
    aux_ref[8:16] = 1.0 / (1.0 - jnp.full(shape, sine * sine))
    aux_ref[16:] = jnp.full(shape, count)
    weight = jnp.where(waves == 0, 1.0, jnp.where(2 * waves < count, 2.0, 0.0))[:1]
    inverse = 1.0 / jnp.full(shape, count)[:1]
    waves, imag = waves[:1], imag[:1]
    tiles = NLON // LANES
    coarse_cos, coarse_sin = cos_sin(
        waves * (LANES * iota((tiles, lanes), 0)).astype(F32), count, inverse
    )
    fine_cos, fine_sin = cos_sin(waves * iota((LANES, lanes), 0).astype(F32), count, inverse)
    coarse_ref[0], coarse_ref[1] = coarse_cos * weight, coarse_sin * weight
    first = jnp.where(imag, -fine_sin, fine_cos)
    second = jnp.where(imag, -fine_cos, -fine_sin)
    for t in range(tiles):
        a, b = coarse_ref[0, t : t + 1], coarse_ref[1, t : t + 1]
        basis_ref[t * LANES : (t + 1) * LANES] = (a * first + b * second).astype(BF16)


def front_kernel(
    sizes,
    counts_hbm,
    sine_hbm,
    pair_hbm,
    legendre_hbm,
    slope_hbm,
    ops_hbm,
    spectral_hbm,
    send_ref,
    basis_ref,
    aux_ref,
    counts_ref,
    sine_ref,
    pair_ref,
    legendre_ref,
    slope_ref,
    ops_ref,
    spectral_ref,
    table_ref,
    joined_ref,
    coarse_ref,
    arrived,
):
    level_ranks, levels_out, pad, total_waves = sizes
    pairs, fields, parts, width, levels = spectral_ref.shape
    _, orders, lats, full = legendre_ref.shape
    half = full // 2
    rank, row = lax.axis_index("lev"), lax.axis_index("wave")
    first_pair = row * pairs
    sub = pairs * orders
    rows = orders * lats
    copies = [
        pltpu.make_async_copy(source, target, arrived.at[index])
        for index, (source, target) in enumerate(
            [
                (counts_hbm, counts_ref),
                (sine_hbm, sine_ref),
                (pair_hbm, pair_ref),
                (legendre_hbm, legendre_ref),
                (slope_hbm, slope_ref),
                (ops_hbm, ops_ref),
            ]
            + [(spectral_hbm.at[:, f], spectral_ref.at[:, f]) for f in range(fields)]
        )
    ]
    for copy in copies:
        copy.start()

    for copy in copies[:3]:
        copy.wait()
    north = lax.rem(row, lats)
    sine = jnp.where(row < lats, sine_ref[north], -sine_ref[north])
    count = counts_ref[row].astype(F32)
    zonal = (pairs, orders, parts, total_waves)
    zonal_tables(zonal, count, sine, pair_ref, basis_ref, aux_ref, coarse_ref)

    for copy in copies[3:]:
        copy.wait()
    for t, ref in enumerate((legendre_ref, slope_ref)):
        for s in range(pairs):
            for w in range(orders):
                base = ((t * pairs + s) * orders + w) * lats
                table_ref[base : base + lats, :] = ref[s, w].astype(F32)
    table = table_ref[...]
    piece = table[:, :width]
    for b in range(1, level_ranks):
        piece = jnp.where(rank == b, table[:, b * width : (b + 1) * width], piece)
    shape = piece.shape
    r, position = iota(shape, 0), rank * width + iota(shape, 1)
    slot, order = (r // rows) % pairs, (r // lats) % orders
    number = jnp.zeros(shape, jnp.int32)
    for s in range(pairs):
        number = jnp.where(slot == s, pair_ref[first_pair + s], number)
    upper = (position >= half).astype(jnp.int32)
    offset = position - half * upper
    count0 = (total_waves - number + 1 - upper) >> 1
    count1 = (number + 2 - upper) >> 1
    low = jnp.where(order == 0, 0, count0)
    high = jnp.where(order == 0, count0, count0 + count1)
    piece = jnp.where((offset >= low) & (offset < high), piece, 0.0)
    plain = [piece[s * rows : (s + 1) * rows] for s in range(pairs)]
    slope = [piece[(pairs + s) * rows : (pairs + s + 1) * rows] for s in range(pairs)]
    both = [jnp.concatenate([a, b], axis=0).astype(BF16) for a, b in zip(plain, slope)]
    plain = [a.astype(BF16) for a in plain]

    sums = [[] for _ in range(FIELDS)]
    for f in range(fields):
        field = spectral_ref[:, f].reshape(pairs * parts * width, levels)
        vertical = dot(field, ops_ref[f], NT).astype(BF16)
        for c in range(parts):
            for s in range(pairs):
                start = (s * parts + c) * width
                block = vertical[start : start + width]
                if f == 2:
                    result = dot(both[s], block)
                    sums[2].append(result[rows:])
                    sums[3].append(result[:rows])
                else:
                    sums[f].append(dot(plain[s], block))

    sums = [jnp.concatenate(x, axis=0) for x in sums]
    sums = [jnp.pad(x, ((0, 0), (0, LANES - levels))) for x in sums]
    sums = [pltpu.roll(x, g * pad, 1) if g else x for g, x in enumerate(sums)]
    lane = iota(sums[0].shape, 1)
    south = jnp.where(rank * width < half, 1.0, -1.0)
    piece_rows = parts * sub
    factor = jnp.where(iota((piece_rows, LANES), 1) // pad == 2, -south, south)
    for d in range(level_ranks):
        shift = d * levels_out
        lane_field = ((lane + (LANES - shift)) % LANES) // pad
        joined = sums[FIELDS - 1]
        for g in range(FIELDS - 1):
            joined = jnp.where(lane_field == g, sums[g], joined)
        if shift:
            joined = pltpu.roll(joined, LANES - shift, 1)
        joined_ref[d] = joined
        for j in range(lats):
            own = joined_ref[d, pl.ds(j, piece_rows, stride=lats), :]
            send_ref[j * level_ranks + d] = own.astype(BF16)
            send_ref[(lats + j) * level_ranks + d] = (own * factor).astype(BF16)


def grid_kernel(sizes, received_ref, basis_ref, aux_ref, out_hbm, out_ref, sent):
    level_ranks, levels_out, pad, group, total_waves = sizes
    chunks, chunk_rows, lanes = received_ref.shape
    sources = chunks // level_ranks
    data = received_ref[...].astype(F32).reshape(sources, level_ranks, chunk_rows, lanes)
    total = jnp.sum(data, axis=1)

    by_level = total.reshape(sources * chunk_rows, lanes).T
    keep = -(-levels_out // 8) * 8
    coeffs = [by_level[g * pad : g * pad + keep] for g in range(FIELDS)]
    zonal = coeffs[3]
    span = zonal.shape[1]
    imag = (iota(zonal.shape, 1) // group) % 2 == 1
    swapped = jnp.where(imag, pltpu.roll(zonal, group, 1), pltpu.roll(zonal, span - group, 1))
    coeffs[3] = swapped * aux_ref[:1]
    coeffs = jnp.concatenate(coeffs, axis=0).astype(BF16)

    inverse, count = aux_ref[8:9, :1], aux_ref[16:17, :1]
    copies = []
    for start in range(0, NLON, COLS):
        values = dot(coeffs, basis_ref[start : start + COLS], NT)
        first, second, third, fourth = (values[g * keep : g * keep + levels_out] for g in range(4))
        result = -(first * fourth * inverse + second * third * (1.0 / total_waves))
        inside = (start + iota(result.shape, 1)).astype(F32) < count
        window = (slice(None), slice(None), slice(start, start + COLS))
        out_ref[:, 0, start : start + COLS] = jnp.where(inside, result, 0.0)
        copy = pltpu.make_async_copy(
            out_ref.at[window], out_hbm.at[window], sent.at[start // COLS]
        )
        copy.start()
        copies.append(copy)
    for copy in copies:
        copy.wait()


def per_device(spectral, vertical_ops, legendre, legendre_slope, sine_lat, pair_map, lon_counts):
    pairs, fields, parts, levels, width = spectral.shape
    level_ranks = lax.axis_size("lev")
    rows = lax.axis_size("wave")
    slots = pair_map.shape[0]
    total_waves = 2 * slots
    levels_out = levels // level_ranks
    pad = LANES // FIELDS
    lats, full = legendre.shape[2:]
    orders = legendre.shape[1]
    group = pairs * orders
    assert rows == 2 * lats == lon_counts.shape[0]
    assert levels_out <= pad and levels <= LANES
    assert (full // 2) % width == 0

    vmem = pl.BlockSpec(memory_space=pltpu.VMEM)
    hbm = pl.BlockSpec(memory_space=pl.ANY)
    by_position = jnp.transpose(spectral, (0, 1, 2, 4, 3))
    resident = 4 * slots * NLON * 2 <= RESIDENT
    placed = pltpu.VMEM if resident else jax.ShapeDtypeStruct
    sources = [lon_counts, sine_lat, pair_map]
    sources += [legendre, legendre_slope, vertical_ops, by_position]
    spaces = [pltpu.SMEM] * 3 + [pltpu.VMEM] * 4
    send, basis, aux = pl.pallas_call(
        functools.partial(front_kernel, (level_ranks, levels_out, pad, total_waves)),
        out_shape=[
            pltpu.VMEM((rows * level_ranks, parts * group, LANES), BF16),
            placed((NLON, 2 * parts * slots), BF16),
            pltpu.VMEM((24, 2 * parts * slots), F32),
        ],
        in_specs=[hbm] * len(sources),
        out_specs=[vmem] * 3,
        scratch_shapes=[space(x.shape, x.dtype) for space, x in zip(spaces, sources)]
        + [
            pltpu.VMEM((2 * group * lats, full), F32),
            pltpu.VMEM((level_ranks, parts * group * lats, LANES), F32),
            pltpu.VMEM((2, NLON // LANES, 2 * parts * slots), F32),
            pltpu.SemaphoreType.DMA((len(sources) - 1 + fields,)),
        ],
        name="front",
    )(*sources)
    received = lax.all_to_all(send, ("wave", "lev"), split_axis=0, concat_axis=0, tiled=True)
    received, aux = (
        pltpu.with_memory_space_constraint(x, pltpu.VMEM) for x in (received, aux)
    )
    if resident:
        basis = pltpu.with_memory_space_constraint(basis, pltpu.VMEM)
    return pl.pallas_call(
        functools.partial(grid_kernel, (level_ranks, levels_out, pad, group, total_waves)),
        out_shape=jax.ShapeDtypeStruct((levels_out, 1, NLON), F32),
        in_specs=[vmem, vmem, vmem],
        out_specs=hbm,
        scratch_shapes=[
            pltpu.VMEM((levels_out, 1, NLON), F32),
            pltpu.SemaphoreType.DMA((NLON // COLS,)),
        ],
        name="grid_tendency",
    )(received, basis, aux)


def solution(mesh):
    placed = (
        P("wave", None, None, None, "lev"),
        P(),
        P("wave", None, None, None),
        P("wave", None, None, None),
        P(),
        P(),
        P(),
    )
    return jax.shard_map(
        per_device, mesh=mesh, in_specs=placed, out_specs=P("lev", "wave", None), check_vma=False
    )
```

```python
import functools
import math

import jax
import jax.numpy as jnp
from jax import lax
from jax.experimental import pallas as pl
from jax.experimental.pallas import tpu as pltpu
from jax.sharding import PartitionSpec as P

NLON = 5120
FIELDS = 4
FIELD_OF = (0, 1, 2, 2)
LANES = 128
COLUMNS = (1280, 1280, 1280, 768, 512)
RESIDENT = 4 << 20
RUN = NLON // LANES // 4

F32 = jnp.float32
BF16 = jnp.bfloat16
NT = (((1,), (1,)), ((), ()))


def dot(a, b, dims=(((1,), (0,)), ((), ()))):
    return lax.dot_general(a, b, dims, preferred_element_type=F32)


def iota(shape, dim):
    return lax.broadcasted_iota(jnp.int32, shape, dim)


def cos_sin(products, count, inverse, quarter=0):
    quarters = jnp.floor(products * 4.0 * inverse + 0.5)
    angle = (products * 4.0 - quarters * count) * inverse * (0.5 * math.pi)
    square = angle * angle
    sine = square * (1.0 / 362880.0) - 1.0 / 5040.0
    sine = square * sine + 1.0 / 120.0
    sine = square * sine - 1.0 / 6.0
    sine = angle + angle * (square * sine)
    cosine = square * (1.0 / 40320.0) - 1.0 / 720.0
    cosine = square * cosine + 1.0 / 24.0
    cosine = square * cosine - 0.5
    cosine = square * cosine + 1.0
    turn = (quarters.astype(jnp.int32) + quarter) & 3
    swap = (turn & 1) == 1
    first = jnp.where(swap, sine, cosine)
    second = jnp.where(swap, cosine, sine)
    first = jnp.where((turn == 1) | (turn == 2), -first, first)
    second = jnp.where(turn >= 2, -second, second)
    return first, second


def zonal_rows(sizes, count, sine, pair_ref, aux_ref):
    pairs, orders, parts, total_waves = sizes
    sub = pairs * orders
    shape = (8, aux_ref.shape[1])
    lane = iota(shape, 1)
    slot = (lane // (parts * sub)) * pairs + (lane % sub) // orders
    number = jnp.zeros(shape, jnp.int32)
    for index in range(total_waves // 2):
        number = jnp.where(slot == index, pair_ref[index], number)
    waves = jnp.where(lane % orders == 1, total_waves - 1 - number, number).astype(F32)
    imag = (lane // sub) % parts
    scale = 1.0 / (1.0 - jnp.full(shape, sine * sine)) / total_waves
    aux_ref[:8] = waves
    aux_ref[8:16] = jnp.where(imag == 1, -waves, waves) * scale
    aux_ref[16:] = jnp.full(shape, count)


def zonal_table(group, aux_ref, rows_ref, fine_ref, basis_ref):
    waves, count = aux_ref[:8], aux_ref[16:]
    shape = waves.shape
    lanes = shape[1]
    weight = jnp.where(waves == 0, 1.0, jnp.where(2 * waves < count, 2.0, 0.0))
    inverse = 1.0 / count
    index = iota(shape, 0)
    tile = (index // 2) * RUN + index % 2
    cosine, sine_part = cos_sin(waves * (tile * LANES).astype(F32), count, inverse)
    rows_ref[0], rows_ref[1] = cosine * weight, sine_part * weight
    rows_ref[2] = 2.0 * cosine
    groups = LANES // 8
    index = iota((groups, lanes), 0)
    cosine, sine_part = cos_sin(waves[:1] * (8 * index).astype(F32), count[:1], inverse[:1])
    rows_ref[3 : 3 + groups // 8] = cosine.reshape(groups // 8, 8, lanes)
    rows_ref[3 + groups // 8 :] = sine_part.reshape(groups // 8, 8, lanes)
    imag = (iota(shape, 1) // group) % 2
    lower_cos, lower_sin = cos_sin(waves * iota(shape, 0).astype(F32), count, inverse, imag)
    for g in range(groups):
        upper = pl.ds(g % 8, 1)
        c, s = rows_ref[3 + g // 8, upper], rows_ref[3 + groups // 8 + g // 8, upper]
        fine_ref[0, 8 * g : 8 * g + 8] = c * lower_cos - s * lower_sin
        fine_ref[1, 8 * g : 8 * g + 8] = -(s * lower_cos + c * lower_sin)
    def one(run, carry):
        zonal_run(run, rows_ref, fine_ref, basis_ref)
        return carry

    lax.fori_loop(0, NLON // LANES // RUN, one, 0)


def zonal_run(run, rows_ref, fine_ref, basis_ref):
    twice = rows_ref[2, 1:2]

    def first(t):
        a, b = rows_ref[0, pl.ds(2 * run + t, 1)], rows_ref[1, pl.ds(2 * run + t, 1)]
        return a * fine_ref[0] + b * fine_ref[1]

    def store(t, tile):
        start = pl.multiple_of((run * RUN + t) * LANES, LANES)
        basis_ref[pl.ds(start, LANES)] = tile.astype(BF16)

    before, here = first(0), first(1)
    store(0, before)
    store(1, here)
    for t in range(2, RUN):
        before, here = here, twice * here - before
        store(t, here)


def table_early():
    return 2 * lax.axis_index("wave") < lax.axis_size("wave")


def front_kernel(
    sizes,
    counts_hbm,
    sine_hbm,
    pair_hbm,
    legendre_hbm,
    slope_hbm,
    ops_hbm,
    spectral_hbm,
    send_ref,
    basis_ref,
    aux_ref,
    counts_ref,
    sine_ref,
    pair_ref,
    legendre_ref,
    slope_ref,
    ops_ref,
    spectral_ref,
    table_ref,
    joined_ref,
    rows_ref,
    fine_ref,
    arrived,
):
    level_ranks, levels_out, pad, total_waves = sizes
    pairs, fields, parts, width, levels = spectral_ref.shape
    _, orders, lats, full = legendre_ref.shape
    half = full // 2
    rank, row = lax.axis_index("lev"), lax.axis_index("wave")
    first_pair = row * pairs
    sub = pairs * orders
    rows = orders * lats
    copies = [
        pltpu.make_async_copy(source, target, arrived.at[index])
        for index, (source, target) in enumerate(
            [
                (counts_hbm, counts_ref),
                (sine_hbm, sine_ref),
                (pair_hbm, pair_ref),
                (legendre_hbm, legendre_ref),
                (slope_hbm, slope_ref),
                (ops_hbm, ops_ref),
            ]
            + [(spectral_hbm.at[:, f], spectral_ref.at[:, f]) for f in range(fields)]
        )
    ]
    for copy in copies:
        copy.start()

    for copy in copies[:3]:
        copy.wait()
    north = lax.rem(row, lats)
    sine = jnp.where(row < lats, sine_ref[north], -sine_ref[north])
    count = counts_ref[row].astype(F32)
    zonal = (pairs, orders, parts, total_waves)
    zonal_rows(zonal, count, sine, pair_ref, aux_ref)

    for copy in copies[3:5]:
        copy.wait()
    for t, ref in enumerate((legendre_ref, slope_ref)):
        for s in range(pairs):
            for w in range(orders):
                base = ((t * pairs + s) * orders + w) * lats
                table_ref[base : base + lats, :] = ref[s, w].astype(F32)
    table = table_ref[...]
    piece = table[:, :width]
    for b in range(1, level_ranks):
        piece = jnp.where(rank == b, table[:, b * width : (b + 1) * width], piece)
    shape = piece.shape
    r, position = iota(shape, 0), rank * width + iota(shape, 1)
    slot, order = (r // rows) % pairs, (r // lats) % orders
    number = jnp.zeros(shape, jnp.int32)
    for s in range(pairs):
        number = jnp.where(slot == s, pair_ref[first_pair + s], number)
    upper = (position >= half).astype(jnp.int32)
    offset = position - half * upper
    count0 = (total_waves - number + 1 - upper) >> 1
    count1 = (number + 2 - upper) >> 1
    low = jnp.where(order == 0, 0, count0)
    high = jnp.where(order == 0, count0, count0 + count1)
    piece = jnp.where((offset >= low) & (offset < high), piece, 0.0)
    plain = [piece[s * rows : (s + 1) * rows] for s in range(pairs)]
    slope = [piece[(pairs + s) * rows : (pairs + s + 1) * rows] for s in range(pairs)]
    both = [jnp.concatenate([a, b], axis=0).astype(BF16) for a, b in zip(plain, slope)]
    plain = [a.astype(BF16) for a in plain]

    copies[5].wait()
    operators = []
    for g, f in enumerate(FIELD_OF):
        padded = jnp.pad(ops_ref[f].astype(F32), ((0, LANES - levels), (0, 0)))
        first = LANES - g * pad
        moved = jnp.concatenate([padded[first:], padded[:first]], axis=0) if g else padded
        operators.append(moved.astype(BF16))

    for copy in copies[6:]:
        copy.wait()
    sums = [[] for _ in range(FIELDS)]
    for f in range(fields):
        for c in range(parts):
            for s in range(pairs):
                block = spectral_ref[s, f, c]
                if f == 2:
                    result = dot(both[s], block)
                    sums[2].append(result[rows:])
                    sums[3].append(result[:rows])
                else:
                    sums[f].append(dot(plain[s], block))

    for g in range(FIELDS):
        exact = jnp.concatenate(sums[g], axis=0)
        high = exact.astype(BF16)
        low = (exact - high.astype(F32)).astype(BF16)
        sums[g] = dot(high, operators[g], NT) + dot(low, operators[g], NT)
    lane = iota(sums[0].shape, 1)
    south = jnp.where(rank * width < half, 1.0, -1.0)
    piece_rows = parts * sub
    factor = jnp.where(iota((piece_rows, LANES), 1) // pad == 2, -south, south)
    for d in range(level_ranks):
        shift = d * levels_out
        lane_field = ((lane + (LANES - shift)) % LANES) // pad
        joined = sums[FIELDS - 1]
        for g in range(FIELDS - 1):
            joined = jnp.where(lane_field == g, sums[g], joined)
        if shift:
            joined = pltpu.roll(joined, LANES - shift, 1)
        joined_ref[d] = joined
        for j in range(lats):
            own = joined_ref[d, pl.ds(j, piece_rows, stride=lats), :]
            send_ref[j * level_ranks + d] = own.astype(BF16)
            send_ref[(lats + j) * level_ranks + d] = (own * factor).astype(BF16)

    @pl.when(table_early())
    def _():
        zonal_table(sub, aux_ref, rows_ref, fine_ref, basis_ref)


def grid_kernel(
    sizes, received_ref, early_ref, aux_ref, out_hbm, basis_ref, out_ref, rows_ref, fine_ref, sent
):
    level_ranks, levels_out, pad, group, total_waves = sizes

    @pl.when(jnp.logical_not(table_early()))
    def _():
        zonal_table(group, aux_ref, rows_ref, fine_ref, basis_ref)

    chunks, chunk_rows, lanes = received_ref.shape
    sources = chunks // level_ranks
    data = received_ref[...].astype(F32).reshape(sources, level_ranks, chunk_rows, lanes)
    total = jnp.sum(data, axis=1)

    by_level = total.reshape(sources * chunk_rows, lanes).T
    keep = -(-levels_out // 8) * 8
    coeffs = [by_level[g * pad : g * pad + keep] for g in range(FIELDS)]
    zonal = coeffs[3]
    span = zonal.shape[1]
    imag = (iota(zonal.shape, 1) // group) % 2 == 1
    swapped = jnp.where(imag, pltpu.roll(zonal, group, 1), pltpu.roll(zonal, span - group, 1))
    coeffs[3] = swapped * aux_ref[8:9]
    coeffs[1] = coeffs[1] * (-1.0 / total_waves)
    coeffs = jnp.concatenate(coeffs, axis=0).astype(BF16)

    count = aux_ref[16:17, :LANES].astype(jnp.int32)
    copies = []
    start = 0
    for index, size in enumerate(COLUMNS):
        values = dot(coeffs, basis_ref[start : start + size], NT)
        first, second, third, fourth = (values[g * keep : g * keep + levels_out] for g in range(4))
        result = first * fourth + second * third
        inside = start + iota((1, size), 1) < count[:, :1]
        window = (slice(None), slice(None), slice(start, start + size))
        out_ref[:, 0, start : start + size] = jnp.where(inside, result, 0.0)
        copy = pltpu.make_async_copy(
            out_ref.at[window], out_hbm.at[window], sent.at[index]
        )
        copy.start()
        copies.append(copy)
        start += size
    for copy in copies:
        copy.wait()


def per_device(spectral, vertical_ops, legendre, legendre_slope, sine_lat, pair_map, lon_counts):
    pairs, fields, parts, levels, width = spectral.shape
    level_ranks = lax.axis_size("lev")
    rows = lax.axis_size("wave")
    slots = pair_map.shape[0]
    total_waves = 2 * slots
    levels_out = levels // level_ranks
    pad = LANES // FIELDS
    lats, full = legendre.shape[2:]
    orders = legendre.shape[1]
    group = pairs * orders
    assert rows == 2 * lats == lon_counts.shape[0]
    assert levels_out <= pad and levels <= LANES
    assert (full // 2) % width == 0

    vmem = pl.BlockSpec(memory_space=pltpu.VMEM)
    hbm = pl.BlockSpec(memory_space=pl.ANY)
    by_position = jnp.transpose(spectral, (0, 1, 2, 4, 3))
    resident = 4 * slots * NLON * 2 <= RESIDENT
    placed = pltpu.VMEM if resident else jax.ShapeDtypeStruct
    sources = [lon_counts, sine_lat, pair_map]
    sources += [legendre, legendre_slope, vertical_ops, by_position]
    tables = [
        pltpu.VMEM((3 + LANES // 32, 8, 2 * parts * slots), F32),
        pltpu.VMEM((2, LANES, 2 * parts * slots), F32),
    ]
    spaces = [pltpu.SMEM] * 3 + [pltpu.VMEM] * 4
    send, basis, aux = pl.pallas_call(
        functools.partial(front_kernel, (level_ranks, levels_out, pad, total_waves)),
        out_shape=[
            pltpu.VMEM((rows * level_ranks, parts * group, LANES), BF16),
            placed((NLON, 2 * parts * slots), BF16),
            pltpu.VMEM((24, 2 * parts * slots), F32),
        ],
        in_specs=[hbm] * len(sources),
        out_specs=[vmem] * 3,
        scratch_shapes=[space(x.shape, x.dtype) for space, x in zip(spaces, sources)]
        + [
            pltpu.VMEM((2 * group * lats, full), F32),
            pltpu.VMEM((level_ranks, parts * group * lats, LANES), F32),
            *tables,
            pltpu.SemaphoreType.DMA((len(sources) - 1 + fields,)),
        ],
        name="front",
    )(*sources)
    received = lax.all_to_all(send, ("wave", "lev"), split_axis=0, concat_axis=0, tiled=True)
    received, aux = (
        pltpu.with_memory_space_constraint(x, pltpu.VMEM) for x in (received, aux)
    )
    if resident:
        basis = pltpu.with_memory_space_constraint(basis, pltpu.VMEM)
    tendency, _ = pl.pallas_call(
        functools.partial(grid_kernel, (level_ranks, levels_out, pad, group, total_waves)),
        out_shape=[
            jax.ShapeDtypeStruct((levels_out, 1, NLON), F32),
            placed((NLON, 2 * parts * slots), BF16),
        ],
        in_specs=[vmem, vmem, vmem],
        out_specs=[hbm, vmem],
        input_output_aliases={1: 1},
        scratch_shapes=[
            pltpu.VMEM((levels_out, 1, NLON), F32),
            *tables,
            pltpu.SemaphoreType.DMA((len(COLUMNS),)),
        ],
        name="grid_tendency",
    )(received, basis, aux)
    return tendency


def solution(mesh):
    placed = (
        P("wave", None, None, None, "lev"),
        P(),
        P("wave", None, None, None),
        P("wave", None, None, None),
        P(),
        P(),
        P(),
    )
    return jax.shard_map(
        per_device, mesh=mesh, in_specs=placed, out_specs=P("lev", "wave", None), check_vma=False
    )
```

```python
import functools
import math

import jax
import jax.numpy as jnp
from jax import lax
from jax.experimental import pallas as pl
from jax.experimental.pallas import tpu as pltpu
from jax.sharding import PartitionSpec as P

NLON = 5120
FIELDS = 4
FIELD_OF = (0, 1, 2, 2)
MAIN = 16
REST = 2
LANES = 128
COLUMNS = (1280, 1280, 1280, 768, 512)
RESIDENT = 4 << 20
RUN = NLON // LANES // 4

F32 = jnp.float32
BF16 = jnp.bfloat16
NT = (((1,), (1,)), ((), ()))


def dot(a, b, dims=(((1,), (0,)), ((), ()))):
    return lax.dot_general(a, b, dims, preferred_element_type=F32)


def iota(shape, dim):
    return lax.broadcasted_iota(jnp.int32, shape, dim)


def cos_sin(products, count, inverse, quarter=0):
    quarters = jnp.floor(products * 4.0 * inverse + 0.5)
    angle = (products * 4.0 - quarters * count) * inverse * (0.5 * math.pi)
    square = angle * angle
    sine = square * (1.0 / 362880.0) - 1.0 / 5040.0
    sine = square * sine + 1.0 / 120.0
    sine = square * sine - 1.0 / 6.0
    sine = angle + angle * (square * sine)
    cosine = square * (1.0 / 40320.0) - 1.0 / 720.0
    cosine = square * cosine + 1.0 / 24.0
    cosine = square * cosine - 0.5
    cosine = square * cosine + 1.0
    turn = (quarters.astype(jnp.int32) + quarter) & 3
    swap = (turn & 1) == 1
    first = jnp.where(swap, sine, cosine)
    second = jnp.where(swap, cosine, sine)
    first = jnp.where((turn == 1) | (turn == 2), -first, first)
    second = jnp.where(turn >= 2, -second, second)
    return first, second


def zonal_rows(sizes, count, sine, pair_ref, aux_ref):
    pairs, orders, parts, total_waves = sizes
    shape = (8, aux_ref.shape[1])
    sources = total_waves // 2 // pairs
    lane = iota(shape, 1)
    slot = (lane % sources) * pairs + (lane // (sources * orders)) % pairs
    number = jnp.zeros(shape, jnp.int32)
    for index in range(total_waves // 2):
        number = jnp.where(slot == index, pair_ref[index], number)
    second = (lane // sources) % orders == 1
    waves = jnp.where(second, total_waves - 1 - number, number).astype(F32)
    imag = lane // (shape[1] // parts)
    scale = 1.0 / (1.0 - jnp.full(shape, sine * sine)) / total_waves
    aux_ref[:8] = waves
    aux_ref[8:16] = jnp.where(imag == 1, -waves, waves) * scale
    aux_ref[16:] = jnp.full(shape, count)


def zonal_table(aux_ref, rows_ref, fine_ref, basis_ref):
    waves, count = aux_ref[:8], aux_ref[16:]
    shape = waves.shape
    lanes = shape[1]
    weight = jnp.where(waves == 0, 1.0, jnp.where(2 * waves < count, 2.0, 0.0))
    inverse = 1.0 / count
    index = iota(shape, 0)
    tile = (index // 2) * RUN + index % 2
    cosine, sine_part = cos_sin(waves * (tile * LANES).astype(F32), count, inverse)
    rows_ref[0], rows_ref[1] = cosine * weight, sine_part * weight
    rows_ref[2] = 2.0 * cosine
    groups = LANES // 8
    index = iota((groups, lanes), 0)
    cosine, sine_part = cos_sin(waves[:1] * (8 * index).astype(F32), count[:1], inverse[:1])
    rows_ref[3 : 3 + groups // 8] = cosine.reshape(groups // 8, 8, lanes)
    rows_ref[3 + groups // 8 :] = sine_part.reshape(groups // 8, 8, lanes)
    imag = iota(shape, 1) // (lanes // 2)
    lower_cos, lower_sin = cos_sin(waves * iota(shape, 0).astype(F32), count, inverse, imag)
    for g in range(groups):
        upper = pl.ds(g % 8, 1)
        c, s = rows_ref[3 + g // 8, upper], rows_ref[3 + groups // 8 + g // 8, upper]
        fine_ref[0, 8 * g : 8 * g + 8] = c * lower_cos - s * lower_sin
        fine_ref[1, 8 * g : 8 * g + 8] = -(s * lower_cos + c * lower_sin)
    def one(run, carry):
        zonal_run(run, rows_ref, fine_ref, basis_ref)
        return carry

    lax.fori_loop(0, NLON // LANES // RUN, one, 0)


def zonal_run(run, rows_ref, fine_ref, basis_ref):
    twice = rows_ref[2, 1:2]

    def first(t):
        a, b = rows_ref[0, pl.ds(2 * run + t, 1)], rows_ref[1, pl.ds(2 * run + t, 1)]
        return a * fine_ref[0] + b * fine_ref[1]

    def store(t, tile):
        start = pl.multiple_of((run * RUN + t) * LANES, LANES)
        basis_ref[pl.ds(start, LANES)] = tile.astype(BF16)

    before, here = first(0), first(1)
    store(0, before)
    store(1, here)
    for t in range(2, RUN):
        before, here = here, twice * here - before
        store(t, here)


def table_early():
    return 2 * lax.axis_index("wave") < lax.axis_size("wave")


def front_kernel(
    sizes,
    counts_hbm,
    sine_hbm,
    pair_hbm,
    legendre_hbm,
    slope_hbm,
    ops_hbm,
    spectral_hbm,
    send_ref,
    basis_ref,
    aux_ref,
    counts_ref,
    sine_ref,
    pair_ref,
    legendre_ref,
    slope_ref,
    ops_ref,
    spectral_ref,
    table_ref,
    main_ref,
    rest_ref,
    rows_ref,
    fine_ref,
    arrived,
):
    level_ranks, levels_out, total_waves = sizes
    pairs, fields, parts, width, levels = spectral_ref.shape
    _, orders, lats, full = legendre_ref.shape
    half = full // 2
    rank, row = lax.axis_index("lev"), lax.axis_index("wave")
    first_pair = row * pairs
    sub = pairs * orders
    rows = orders * lats
    copies = [
        pltpu.make_async_copy(source, target, arrived.at[index])
        for index, (source, target) in enumerate(
            [
                (counts_hbm, counts_ref),
                (sine_hbm, sine_ref),
                (pair_hbm, pair_ref),
                (legendre_hbm, legendre_ref),
                (slope_hbm, slope_ref),
                (ops_hbm, ops_ref),
            ]
            + [(spectral_hbm.at[:, f], spectral_ref.at[:, f]) for f in range(fields)]
        )
    ]
    for copy in copies:
        copy.start()

    rest = levels_out - min(levels_out, MAIN)
    shape = (level_ranks * MAIN, levels)
    r, level = iota(shape, 0), iota(shape, 1)
    wanted = (r // MAIN) * levels_out + MAIN + r % REST
    chosen = (level == wanted) & (r % REST < rest)
    places = [(chosen & ((r % MAIN) // REST == g)).astype(F32).astype(BF16) for g in range(FIELDS)]

    for copy in copies[:3]:
        copy.wait()
    north = lax.rem(row, lats)
    sine = jnp.where(row < lats, sine_ref[north], -sine_ref[north])
    count = counts_ref[row].astype(F32)
    zonal = (pairs, orders, parts, total_waves)
    zonal_rows(zonal, count, sine, pair_ref, aux_ref)

    for copy in copies[3:5]:
        copy.wait()
    for t, ref in enumerate((legendre_ref, slope_ref)):
        for s in range(pairs):
            for w in range(orders):
                base = ((t * pairs + s) * orders + w) * lats
                table_ref[base : base + lats, :] = ref[s, w].astype(F32)
    table = table_ref[...]
    piece = table[:, :width]
    for b in range(1, level_ranks):
        piece = jnp.where(rank == b, table[:, b * width : (b + 1) * width], piece)
    shape = piece.shape
    r, position = iota(shape, 0), rank * width + iota(shape, 1)
    slot, order = (r // rows) % pairs, (r // lats) % orders
    number = jnp.zeros(shape, jnp.int32)
    for s in range(pairs):
        number = jnp.where(slot == s, pair_ref[first_pair + s], number)
    upper = (position >= half).astype(jnp.int32)
    offset = position - half * upper
    count0 = (total_waves - number + 1 - upper) >> 1
    count1 = (number + 2 - upper) >> 1
    low = jnp.where(order == 0, 0, count0)
    high = jnp.where(order == 0, count0, count0 + count1)
    piece = jnp.where((offset >= low) & (offset < high), piece, 0.0)
    plain = [piece[s * rows : (s + 1) * rows] for s in range(pairs)]
    slope = [piece[(pairs + s) * rows : (pairs + s + 1) * rows] for s in range(pairs)]
    both = [jnp.concatenate([a, b], axis=0).astype(BF16) for a, b in zip(plain, slope)]
    plain = [a.astype(BF16) for a in plain]

    for copy in copies[5:]:
        copy.wait()
    sums = [[] for _ in range(FIELDS)]
    for f in range(fields):
        for c in range(parts):
            for s in range(pairs):
                block = spectral_ref[s, f, c]
                if f == 2:
                    result = dot(both[s], block)
                    sums[3].append(result[rows:])
                    sums[2].append(result[:rows])
                else:
                    sums[f].append(dot(plain[s], block))

    operators = []
    for g, f in enumerate(FIELD_OF):
        below = LANES - levels - g * MAIN
        pieces = [ops_ref[f], jnp.zeros((below, levels), BF16)]
        if g:
            pieces = [jnp.zeros((g * MAIN, levels), BF16)] + pieces
        if rest:
            pieces.append(dot(places[g], ops_ref[f]).astype(BF16))
            pieces.append(jnp.zeros((LANES - level_ranks * MAIN, levels), BF16))
        operators.append(jnp.concatenate(pieces, axis=0))

    for g in range(FIELDS):
        exact = jnp.concatenate(sums[g], axis=0)
        high = exact.astype(BF16)
        low = (exact - high.astype(F32)).astype(BF16)
        sums[g] = dot(high, operators[g], NT) + dot(low, operators[g], NT)
    count_rows = pairs * rows
    lane = iota((parts * count_rows, LANES), 1)
    right = lane[:count_rows] >= LANES // parts
    south = jnp.where(rank * width < half, 1.0, -1.0)
    factor = jnp.where((iota((sub, LANES), 1) // MAIN) % FIELDS == FIELDS - 1, -south, south)
    for d in range(level_ranks):
        shift = d * levels_out
        joined = sums[0][:, :LANES]
        for g in range(1, FIELDS):
            joined = jnp.where(lane >= shift + g * MAIN, sums[g][:, :LANES], joined)
        real, imag = joined[:count_rows], joined[count_rows:]
        if shift:
            real = pltpu.roll(real, LANES - shift, 1)
        imag = pltpu.roll(imag, (LANES // parts - shift) % LANES, 1)
        main_ref[d] = jnp.where(right, imag, real)
        for j in range(lats):
            own = main_ref[d, pl.ds(j, sub, stride=lats), :]
            shape = (sub // 2, 2, LANES)
            for place, piece in ((j, own), (lats + j, own * factor)):
                send_ref[place * level_ranks + d, : sub // 2] = piece.astype(BF16).reshape(shape)
    if rest:
        block = MAIN
        total = (sums[0] + sums[1] + sums[2] + sums[3])[:, LANES:]
        total = total[:count_rows] + pltpu.roll(total[count_rows:], FIELDS * REST, 1)
        pieces = [total[s * rows : (s + 1) * rows] for s in range(pairs)]
        pieces = [pltpu.roll(x, s * block, 1) if s else x for s, x in enumerate(pieces)]
        lane = iota((rows, LANES), 1)
        lane_field = (iota((orders, LANES), 1) // REST) % FIELDS
        factor = jnp.where(lane_field == FIELDS - 1, -south, south)
        for d in range(level_ranks):
            joined = pieces[0]
            for s in range(1, pairs):
                joined = jnp.where(lane >= (d + s) * block, pieces[s], joined)
            if d:
                joined = pltpu.roll(joined, LANES - d * block, 1)
            rest_ref[d] = joined
            for j in range(lats):
                own = rest_ref[d, pl.ds(j, orders, stride=lats), :]
                for place, piece in ((j, own), (lats + j, own * factor)):
                    send_ref[place * level_ranks + d, sub // 2] = piece.astype(BF16)

    @pl.when(table_early())
    def _():
        zonal_table(aux_ref, rows_ref, fine_ref, basis_ref)


def grid_kernel(
    sizes,
    received_ref,
    early_ref,
    aux_ref,
    out_hbm,
    basis_ref,
    out_ref,
    main_ref,
    rest_ref,
    rows_ref,
    fine_ref,
    sent,
):
    level_ranks, levels_out, pairs, orders, total_waves = sizes
    sub = pairs * orders
    main_levels = min(levels_out, MAIN)
    rest = levels_out - main_levels

    @pl.when(jnp.logical_not(table_early()))
    def _():
        zonal_table(aux_ref, rows_ref, fine_ref, basis_ref)

    sources = received_ref.shape[0] // level_ranks
    half = sub * sources
    derivative = aux_ref[8:9]
    scale = -1.0 / total_waves
    if rest:
        for a in range(sources):
            parts = [received_ref[a * level_ranks + b, sub // 2] for b in range(level_ranks)]
            rest_ref[orders * a : orders * (a + 1)] = sum(x.astype(F32) for x in parts)
        stacked = [rest_ref[pl.ds(w, sources, stride=orders), :] for w in range(orders)]
        turned = jnp.concatenate(stacked, axis=0).T
        block = FIELDS * REST
        pieces = [
            turned[s * MAIN + c * block : s * MAIN + (c + 1) * block]
            for c in range(2)
            for s in range(pairs)
        ]
        extra = jnp.concatenate(pieces, axis=1)
        field = iota(extra.shape, 0) // REST
        swapped = pltpu.roll(extra, half, 1) * derivative
        extra = jnp.where(field == 2, swapped, jnp.where(field == 1, extra * scale, extra))
    for a in range(sources):
        parts = [received_ref[a * level_ranks + b, : sub // 2] for b in range(level_ranks)]
        main_ref[sub * a : sub * (a + 1)] = sum(x.astype(F32) for x in parts).reshape(sub, LANES)
    stacked = [main_ref[pl.ds(i, sources, stride=sub), :] for i in range(sub)]
    turned = jnp.concatenate(stacked, axis=0).T
    coeffs = jnp.concatenate([turned[: LANES // 2], turned[LANES // 2 :]], axis=1)
    coeffs = [coeffs[g * MAIN : (g + 1) * MAIN] for g in range(FIELDS)]
    coeffs[2] = pltpu.roll(coeffs[2], half, 1) * derivative
    coeffs[1] = coeffs[1] * scale
    coeffs = jnp.concatenate(coeffs + ([extra] if rest else []), axis=0).astype(BF16)

    count = aux_ref[16:17, :1].astype(jnp.int32)
    copies = []
    start = 0
    for index, size in enumerate(COLUMNS):
        values = dot(coeffs, basis_ref[start : start + size], NT)
        inside = start + iota((1, size), 1) < count
        first, second, third, slope = (values[g * MAIN : (g + 1) * MAIN] for g in range(FIELDS))
        result = jnp.where(inside, first * third + second * slope, 0.0)
        out_ref[:main_levels, 0, start : start + size] = result[:main_levels]
        if rest:
            value = values[FIELDS * MAIN :]
            product = value * pltpu.roll(value, 2 * REST, 0)
            result = product[:REST] + product[REST : 2 * REST]
            result = jnp.where(inside, result, 0.0)
            out_ref[main_levels:, 0, start : start + size] = result[:rest]
        window = (slice(None), slice(None), slice(start, start + size))
        copy = pltpu.make_async_copy(out_ref.at[window], out_hbm.at[window], sent.at[index])
        copy.start()
        copies.append(copy)
        start += size
    for copy in copies:
        copy.wait()


def per_device(spectral, vertical_ops, legendre, legendre_slope, sine_lat, pair_map, lon_counts):
    pairs, fields, parts, levels, width = spectral.shape
    level_ranks = lax.axis_size("lev")
    rows = lax.axis_size("wave")
    slots = pair_map.shape[0]
    total_waves = 2 * slots
    levels_out = levels // level_ranks
    lats, full = legendre.shape[2:]
    orders = legendre.shape[1]
    group = pairs * orders
    assert rows == 2 * lats == lon_counts.shape[0]
    rest = max(levels_out - MAIN, 0)
    assert rest <= REST and levels + FIELDS * MAIN - MAIN <= LANES
    assert parts * FIELDS * MAIN == LANES and group % 2 == 0
    assert not rest or level_ranks + pairs - 1 <= LANES // MAIN
    assert (full // 2) % width == 0

    vmem = pl.BlockSpec(memory_space=pltpu.VMEM)
    hbm = pl.BlockSpec(memory_space=pl.ANY)
    by_position = jnp.transpose(spectral, (0, 1, 2, 4, 3))
    resident = 4 * slots * NLON * 2 <= RESIDENT
    placed = pltpu.VMEM if resident else jax.ShapeDtypeStruct
    sources = [lon_counts, sine_lat, pair_map]
    sources += [legendre, legendre_slope, vertical_ops, by_position]
    tables = [
        pltpu.VMEM((3 + LANES // 32, 8, 2 * parts * slots), F32),
        pltpu.VMEM((2, LANES, 2 * parts * slots), F32),
    ]
    spaces = [pltpu.SMEM] * 3 + [pltpu.VMEM] * 4
    send, basis, aux = pl.pallas_call(
        functools.partial(front_kernel, (level_ranks, levels_out, total_waves)),
        out_shape=[
            pltpu.VMEM((rows * level_ranks, group // 2 + (rest > 0), 2, LANES), BF16),
            placed((NLON, 2 * parts * slots), BF16),
            pltpu.VMEM((24, 2 * parts * slots), F32),
        ],
        in_specs=[hbm] * len(sources),
        out_specs=[vmem] * 3,
        scratch_shapes=[space(x.shape, x.dtype) for space, x in zip(spaces, sources)]
        + [
            pltpu.VMEM((2 * group * lats, full), F32),
            pltpu.VMEM((level_ranks, group * lats, LANES), F32),
            pltpu.VMEM((level_ranks, orders * lats, LANES), F32),
            *tables,
            pltpu.SemaphoreType.DMA((len(sources) - 1 + fields,)),
        ],
        name="front",
    )(*sources)
    received = lax.all_to_all(send, ("wave", "lev"), split_axis=0, concat_axis=0, tiled=True)
    received, aux = (
        pltpu.with_memory_space_constraint(x, pltpu.VMEM) for x in (received, aux)
    )
    if resident:
        basis = pltpu.with_memory_space_constraint(basis, pltpu.VMEM)
    tendency, _ = pl.pallas_call(
        functools.partial(grid_kernel, (level_ranks, levels_out, pairs, orders, total_waves)),
        out_shape=[
            jax.ShapeDtypeStruct((levels_out, 1, NLON), F32),
            placed((NLON, 2 * parts * slots), BF16),
        ],
        in_specs=[vmem, vmem, vmem],
        out_specs=[hbm, vmem],
        input_output_aliases={1: 1},
        scratch_shapes=[
            pltpu.VMEM((levels_out, 1, NLON), F32),
            pltpu.VMEM((rows * group, LANES), F32),
            pltpu.VMEM((rows * orders, LANES), F32),
            *tables,
            pltpu.SemaphoreType.DMA((len(COLUMNS),)),
        ],
        name="grid_tendency",
    )(received, basis, aux)
    return tendency


def solution(mesh):
    placed = (
        P("wave", None, None, None, "lev"),
        P(),
        P("wave", None, None, None),
        P("wave", None, None, None),
        P(),
        P(),
        P(),
    )
    return jax.shard_map(
        per_device, mesh=mesh, in_specs=placed, out_specs=P("lev", "wave", None), check_vma=False
    )
```

```python
import functools
import math

import jax
import jax.numpy as jnp
from jax import lax
from jax.experimental import pallas as pl
from jax.experimental.pallas import tpu as pltpu
from jax.sharding import PartitionSpec as P

NLON = 5120
FIELDS = 4
FIELD_OF = (0, 1, 2, 2)
MAIN = 16
REST = 2
LANES = 128
COLUMNS = (1280, 1280, 1280, 768, 512)
RESIDENT = 4 << 20
RUN = NLON // LANES // 4

F32 = jnp.float32
BF16 = jnp.bfloat16
NT = (((1,), (1,)), ((), ()))


def dot(a, b, dims=(((1,), (0,)), ((), ()))):
    return lax.dot_general(a, b, dims, preferred_element_type=F32)


def iota(shape, dim):
    return lax.broadcasted_iota(jnp.int32, shape, dim)


def cos_sin(products, count, inverse, quarter=0):
    quarters = jnp.floor(products * 4.0 * inverse + 0.5)
    angle = (products * 4.0 - quarters * count) * inverse * (0.5 * math.pi)
    square = angle * angle
    sine = square * (1.0 / 362880.0) - 1.0 / 5040.0
    sine = square * sine + 1.0 / 120.0
    sine = square * sine - 1.0 / 6.0
    sine = angle + angle * (square * sine)
    cosine = square * (1.0 / 40320.0) - 1.0 / 720.0
    cosine = square * cosine + 1.0 / 24.0
    cosine = square * cosine - 0.5
    cosine = square * cosine + 1.0
    turn = (quarters.astype(jnp.int32) + quarter) & 3
    swap = (turn & 1) == 1
    first = jnp.where(swap, sine, cosine)
    second = jnp.where(swap, cosine, sine)
    first = jnp.where((turn == 1) | (turn == 2), -first, first)
    second = jnp.where(turn >= 2, -second, second)
    return first, second


def zonal_rows(sizes, count, sine, pair_ref, aux_ref):
    pairs, orders, parts, total_waves = sizes
    shape = (8, aux_ref.shape[1])
    sources = total_waves // 2 // pairs
    lane = iota(shape, 1)
    slot = (lane % sources) * pairs + (lane // (sources * orders)) % pairs
    number = jnp.zeros(shape, jnp.int32)
    for index in range(total_waves // 2):
        number = jnp.where(slot == index, pair_ref[index], number)
    second = (lane // sources) % orders == 1
    waves = jnp.where(second, total_waves - 1 - number, number).astype(F32)
    imag = lane // (shape[1] // parts)
    scale = 1.0 / (1.0 - jnp.full(shape, sine * sine)) / total_waves
    aux_ref[:8] = waves
    aux_ref[8:16] = jnp.where(imag == 1, -waves, waves) * scale
    aux_ref[16:] = jnp.full(shape, count)


def zonal_table(aux_ref, rows_ref, fine_ref, basis_ref):
    waves, count = aux_ref[:8], aux_ref[16:]
    shape = waves.shape
    lanes = shape[1]
    weight = jnp.where(waves == 0, 1.0, jnp.where(2 * waves < count, 2.0, 0.0))
    inverse = 1.0 / count
    index = iota(shape, 0)
    tile = (index // 2) * RUN + index % 2
    cosine, sine_part = cos_sin(waves * (tile * LANES).astype(F32), count, inverse)
    rows_ref[0], rows_ref[1] = cosine * weight, sine_part * weight
    rows_ref[2] = 2.0 * cosine
    groups = LANES // 8
    index = iota((groups, lanes), 0)
    cosine, sine_part = cos_sin(waves[:1] * (8 * index).astype(F32), count[:1], inverse[:1])
    rows_ref[3 : 3 + groups // 8] = cosine.reshape(groups // 8, 8, lanes)
    rows_ref[3 + groups // 8 :] = sine_part.reshape(groups // 8, 8, lanes)
    imag = iota(shape, 1) // (lanes // 2)
    lower_cos, lower_sin = cos_sin(waves * iota(shape, 0).astype(F32), count, inverse, imag)
    for g in range(groups):
        upper = pl.ds(g % 8, 1)
        c, s = rows_ref[3 + g // 8, upper], rows_ref[3 + groups // 8 + g // 8, upper]
        fine_ref[0, 8 * g : 8 * g + 8] = c * lower_cos - s * lower_sin
        fine_ref[1, 8 * g : 8 * g + 8] = -(s * lower_cos + c * lower_sin)
    def one(run, carry):
        zonal_run(run, rows_ref, fine_ref, basis_ref)
        return carry

    lax.fori_loop(0, NLON // LANES // RUN, one, 0)


def zonal_run(run, rows_ref, fine_ref, basis_ref):
    twice = rows_ref[2, 1:2]

    def first(t):
        a, b = rows_ref[0, pl.ds(2 * run + t, 1)], rows_ref[1, pl.ds(2 * run + t, 1)]
        return a * fine_ref[0] + b * fine_ref[1]

    def store(t, tile):
        start = pl.multiple_of((run * RUN + t) * LANES, LANES)
        basis_ref[pl.ds(start, LANES)] = tile.astype(BF16)

    before, here = first(0), first(1)
    store(0, before)
    store(1, here)
    for t in range(2, RUN):
        before, here = here, twice * here - before
        store(t, here)


def table_early():
    return 2 * lax.axis_index("wave") < lax.axis_size("wave")


def front_kernel(
    sizes,
    counts_hbm,
    sine_hbm,
    pair_hbm,
    legendre_hbm,
    slope_hbm,
    ops_hbm,
    spectral_hbm,
    send_ref,
    basis_ref,
    aux_ref,
    counts_ref,
    sine_ref,
    pair_ref,
    legendre_ref,
    slope_ref,
    ops_ref,
    spectral_ref,
    table_ref,
    main_ref,
    rest_ref,
    rows_ref,
    fine_ref,
    arrived,
):
    level_ranks, levels_out, total_waves = sizes
    pairs, fields, parts, width, levels = spectral_ref.shape
    _, orders, lats, full = legendre_ref.shape
    half = full // 2
    rank, row = lax.axis_index("lev"), lax.axis_index("wave")
    first_pair = row * pairs
    sub = pairs * orders
    rows = orders * lats
    copies = [
        pltpu.make_async_copy(source, target, arrived.at[index])
        for index, (source, target) in enumerate(
            [
                (counts_hbm, counts_ref),
                (sine_hbm, sine_ref),
                (pair_hbm, pair_ref),
                (legendre_hbm, legendre_ref),
                (slope_hbm, slope_ref),
                (ops_hbm, ops_ref),
            ]
            + [(spectral_hbm, spectral_ref)]
        )
    ]
    for copy in copies:
        copy.start()

    rest = levels_out - min(levels_out, MAIN)
    shape = (level_ranks * MAIN, levels)
    r, level = iota(shape, 0), iota(shape, 1)
    wanted = (r // MAIN) * levels_out + MAIN + r % REST
    chosen = (level == wanted) & (r % REST < rest)
    places = [(chosen & ((r % MAIN) // REST == g)).astype(F32).astype(BF16) for g in range(FIELDS)]

    for copy in copies[:3]:
        copy.wait()
    north = lax.rem(row, lats)
    sine = jnp.where(row < lats, sine_ref[north], -sine_ref[north])
    count = counts_ref[row].astype(F32)
    zonal = (pairs, orders, parts, total_waves)
    zonal_rows(zonal, count, sine, pair_ref, aux_ref)

    for copy in copies[3:5]:
        copy.wait()
    for t, ref in enumerate((legendre_ref, slope_ref)):
        for s in range(pairs):
            for w in range(orders):
                base = ((t * pairs + s) * orders + w) * lats
                table_ref[base : base + lats, :] = ref[s, w].astype(F32)
    table = table_ref[...]
    piece = table[:, :width]
    for b in range(1, level_ranks):
        piece = jnp.where(rank == b, table[:, b * width : (b + 1) * width], piece)
    shape = piece.shape
    r, position = iota(shape, 0), rank * width + iota(shape, 1)
    slot, order = (r // rows) % pairs, (r // lats) % orders
    number = jnp.zeros(shape, jnp.int32)
    for s in range(pairs):
        number = jnp.where(slot == s, pair_ref[first_pair + s], number)
    upper = (position >= half).astype(jnp.int32)
    offset = position - half * upper
    count0 = (total_waves - number + 1 - upper) >> 1
    count1 = (number + 2 - upper) >> 1
    low = jnp.where(order == 0, 0, count0)
    high = jnp.where(order == 0, count0, count0 + count1)
    piece = jnp.where((offset >= low) & (offset < high), piece, 0.0)
    plain = [piece[s * rows : (s + 1) * rows] for s in range(pairs)]
    slope = [piece[(pairs + s) * rows : (pairs + s + 1) * rows] for s in range(pairs)]
    both = [jnp.concatenate([a, b], axis=0).astype(BF16) for a, b in zip(plain, slope)]
    plain = [a.astype(BF16) for a in plain]

    for copy in copies[5:]:
        copy.wait()
    sums = [[] for _ in range(FIELDS)]
    for f in range(fields):
        for c in range(parts):
            for s in range(pairs):
                block = spectral_ref[s, f, c]
                if f == 2:
                    result = dot(both[s], block)
                    sums[3].append(result[rows:])
                    sums[2].append(result[:rows])
                else:
                    sums[f].append(dot(plain[s], block))

    operators = []
    for g, f in enumerate(FIELD_OF):
        below = LANES - levels - g * MAIN
        pieces = [ops_ref[f], jnp.zeros((below, levels), BF16)]
        if g:
            pieces = [jnp.zeros((g * MAIN, levels), BF16)] + pieces
        if rest:
            pieces.append(dot(places[g], ops_ref[f]).astype(BF16))
            pieces.append(jnp.zeros((LANES - level_ranks * MAIN, levels), BF16))
        operators.append(jnp.concatenate(pieces, axis=0))

    for g in range(FIELDS):
        exact = jnp.concatenate(sums[g], axis=0)
        high = exact.astype(BF16)
        low = (exact - high.astype(F32)).astype(BF16)
        both_terms = dot(jnp.concatenate([high, low], axis=0), operators[g], NT)
        sums[g] = both_terms[: exact.shape[0]] + both_terms[exact.shape[0] :]
    count_rows = pairs * rows
    lane = iota((parts * count_rows, LANES), 1)
    right = lane[:count_rows] >= LANES // parts
    south = jnp.where(rank * width < half, 1.0, -1.0)
    factor = jnp.where((iota((sub, LANES), 1) // MAIN) % FIELDS == FIELDS - 1, -south, south)
    for d in range(level_ranks):
        shift = d * levels_out
        joined = sums[0][:, :LANES]
        for g in range(1, FIELDS):
            joined = jnp.where(lane >= shift + g * MAIN, sums[g][:, :LANES], joined)
        real, imag = joined[:count_rows], joined[count_rows:]
        if shift:
            real = pltpu.roll(real, LANES - shift, 1)
        imag = pltpu.roll(imag, (LANES // parts - shift) % LANES, 1)
        main_ref[d] = jnp.where(right, imag, real)
        for j in range(lats):
            own = main_ref[d, pl.ds(j, sub, stride=lats), :]
            shape = (sub // 2, 2, LANES)
            for place, piece in ((j, own), (lats + j, own * factor)):
                send_ref[place * level_ranks + d, : sub // 2] = piece.astype(BF16).reshape(shape)
    if rest:
        block = MAIN
        total = (sums[0] + sums[1] + sums[2] + sums[3])[:, LANES:]
        total = total[:count_rows] + pltpu.roll(total[count_rows:], FIELDS * REST, 1)
        pieces = [total[s * rows : (s + 1) * rows] for s in range(pairs)]
        pieces = [pltpu.roll(x, s * block, 1) if s else x for s, x in enumerate(pieces)]
        lane = iota((rows, LANES), 1)
        lane_field = (iota((orders, LANES), 1) // REST) % FIELDS
        factor = jnp.where(lane_field == FIELDS - 1, -south, south)
        for d in range(level_ranks):
            joined = pieces[0]
            for s in range(1, pairs):
                joined = jnp.where(lane >= (d + s) * block, pieces[s], joined)
            if d:
                joined = pltpu.roll(joined, LANES - d * block, 1)
            rest_ref[d] = joined
            for j in range(lats):
                own = rest_ref[d, pl.ds(j, orders, stride=lats), :]
                for place, piece in ((j, own), (lats + j, own * factor)):
                    send_ref[place * level_ranks + d, sub // 2] = piece.astype(BF16)

    @pl.when(table_early())
    def _():
        zonal_table(aux_ref, rows_ref, fine_ref, basis_ref)


def grid_kernel(
    sizes,
    received_ref,
    early_ref,
    aux_ref,
    out_hbm,
    basis_ref,
    out_ref,
    main_ref,
    rest_ref,
    rows_ref,
    fine_ref,
    sent,
):
    level_ranks, levels_out, pairs, orders, total_waves = sizes
    sub = pairs * orders
    main_levels = min(levels_out, MAIN)
    rest = levels_out - main_levels

    @pl.when(jnp.logical_not(table_early()))
    def _():
        zonal_table(aux_ref, rows_ref, fine_ref, basis_ref)

    sources = received_ref.shape[0] // level_ranks
    half = sub * sources
    derivative = aux_ref[8:9]
    scale = -1.0 / total_waves
    if rest:
        for a in range(sources):
            parts = [received_ref[a * level_ranks + b, sub // 2] for b in range(level_ranks)]
            rest_ref[orders * a : orders * (a + 1)] = sum(x.astype(F32) for x in parts)
        stacked = [rest_ref[pl.ds(w, sources, stride=orders), :] for w in range(orders)]
        turned = jnp.concatenate(stacked, axis=0).T
        block = FIELDS * REST
        pieces = [
            turned[s * MAIN + c * block : s * MAIN + (c + 1) * block]
            for c in range(2)
            for s in range(pairs)
        ]
        extra = jnp.concatenate(pieces, axis=1)
        field = iota(extra.shape, 0) // REST
        swapped = pltpu.roll(extra, half, 1) * derivative
        extra = jnp.where(field == 2, swapped, jnp.where(field == 1, extra * scale, extra))
    for a in range(sources):
        parts = [received_ref[a * level_ranks + b, : sub // 2] for b in range(level_ranks)]
        main_ref[sub * a : sub * (a + 1)] = sum(x.astype(F32) for x in parts).reshape(sub, LANES)
    stacked = [main_ref[pl.ds(i, sources, stride=sub), :] for i in range(sub)]
    turned = jnp.concatenate(stacked, axis=0).T
    coeffs = jnp.concatenate([turned[: LANES // 2], turned[LANES // 2 :]], axis=1)
    coeffs = [coeffs[g * MAIN : (g + 1) * MAIN] for g in range(FIELDS)]
    coeffs[2] = pltpu.roll(coeffs[2], half, 1) * derivative
    coeffs[1] = coeffs[1] * scale
    coeffs = jnp.concatenate(coeffs + ([extra] if rest else []), axis=0).astype(BF16)

    count = aux_ref[16:17, :1].astype(jnp.int32)
    copies = []
    start = 0
    for index, size in enumerate(COLUMNS):
        values = dot(coeffs, basis_ref[start : start + size], NT)
        inside = start + iota((1, size), 1) < count
        first, second, third, slope = (values[g * MAIN : (g + 1) * MAIN] for g in range(FIELDS))
        result = jnp.where(inside, first * third + second * slope, 0.0)
        out_ref[:main_levels, 0, start : start + size] = result[:main_levels]
        if rest:
            value = values[FIELDS * MAIN :]
            product = value * pltpu.roll(value, 2 * REST, 0)
            result = product[:REST] + product[REST : 2 * REST]
            result = jnp.where(inside, result, 0.0)
            out_ref[main_levels:, 0, start : start + size] = result[:rest]
        window = (slice(None), slice(None), slice(start, start + size))
        copy = pltpu.make_async_copy(out_ref.at[window], out_hbm.at[window], sent.at[index])
        copy.start()
        copies.append(copy)
        start += size
    for copy in copies:
        copy.wait()


def per_device(spectral, vertical_ops, legendre, legendre_slope, sine_lat, pair_map, lon_counts):
    pairs, fields, parts, levels, width = spectral.shape
    level_ranks = lax.axis_size("lev")
    rows = lax.axis_size("wave")
    slots = pair_map.shape[0]
    total_waves = 2 * slots
    levels_out = levels // level_ranks
    lats, full = legendre.shape[2:]
    orders = legendre.shape[1]
    group = pairs * orders
    assert rows == 2 * lats == lon_counts.shape[0]
    rest = max(levels_out - MAIN, 0)
    assert rest <= REST and levels + FIELDS * MAIN - MAIN <= LANES
    assert parts * FIELDS * MAIN == LANES and group % 2 == 0
    assert not rest or level_ranks + pairs - 1 <= LANES // MAIN
    assert (full // 2) % width == 0

    vmem = pl.BlockSpec(memory_space=pltpu.VMEM)
    hbm = pl.BlockSpec(memory_space=pl.ANY)
    by_position = jnp.transpose(spectral, (0, 1, 2, 4, 3))
    resident = 4 * slots * NLON * 2 <= RESIDENT
    placed = pltpu.VMEM if resident else jax.ShapeDtypeStruct
    sources = [lon_counts, sine_lat, pair_map]
    sources += [legendre, legendre_slope, vertical_ops, by_position]
    tables = [
        pltpu.VMEM((3 + LANES // 32, 8, 2 * parts * slots), F32),
        pltpu.VMEM((2, LANES, 2 * parts * slots), F32),
    ]
    spaces = [pltpu.SMEM] * 3 + [pltpu.VMEM] * 4
    send, basis, aux = pl.pallas_call(
        functools.partial(front_kernel, (level_ranks, levels_out, total_waves)),
        out_shape=[
            pltpu.VMEM((rows * level_ranks, group // 2 + (rest > 0), 2, LANES), BF16),
            placed((NLON, 2 * parts * slots), BF16),
            pltpu.VMEM((24, 2 * parts * slots), F32),
        ],
        in_specs=[hbm] * len(sources),
        out_specs=[vmem] * 3,
        scratch_shapes=[space(x.shape, x.dtype) for space, x in zip(spaces, sources)]
        + [
            pltpu.VMEM((2 * group * lats, full), F32),
            pltpu.VMEM((level_ranks, group * lats, LANES), F32),
            pltpu.VMEM((level_ranks, orders * lats, LANES), F32),
            *tables,
            pltpu.SemaphoreType.DMA((len(sources),)),
        ],
        name="front",
    )(*sources)
    received = lax.all_to_all(send, ("wave", "lev"), split_axis=0, concat_axis=0, tiled=True)
    received, aux = (
        pltpu.with_memory_space_constraint(x, pltpu.VMEM) for x in (received, aux)
    )
    if resident:
        basis = pltpu.with_memory_space_constraint(basis, pltpu.VMEM)
    tendency, _ = pl.pallas_call(
        functools.partial(grid_kernel, (level_ranks, levels_out, pairs, orders, total_waves)),
        out_shape=[
            jax.ShapeDtypeStruct((levels_out, 1, NLON), F32),
            placed((NLON, 2 * parts * slots), BF16),
        ],
        in_specs=[vmem, vmem, vmem],
        out_specs=[hbm, vmem],
        input_output_aliases={1: 1},
        scratch_shapes=[
            pltpu.VMEM((levels_out, 1, NLON), F32),
            pltpu.VMEM((rows * group, LANES), F32),
            pltpu.VMEM((rows * orders, LANES), F32),
            *tables,
            pltpu.SemaphoreType.DMA((len(COLUMNS),)),
        ],
        name="grid_tendency",
    )(received, basis, aux)
    return tendency


def solution(mesh):
    placed = (
        P("wave", None, None, None, "lev"),
        P(),
        P("wave", None, None, None),
        P("wave", None, None, None),
        P(),
        P(),
        P(),
    )
    return jax.shard_map(
        per_device, mesh=mesh, in_specs=placed, out_specs=P("lev", "wave", None), check_vma=False
    )
```

```python
import functools
import math

import jax
import jax.numpy as jnp
from jax import lax
from jax.experimental import pallas as pl
from jax.experimental.pallas import tpu as pltpu
from jax.sharding import PartitionSpec as P

NLON = 5120
FIELDS = 4
FIELD_OF = (0, 1, 2, 2)
MAIN = 16
REST = 2
LANES = 128
COLUMNS = (1280, 1280, 1280, 768, 512)
RESIDENT = 4 << 20
RUN = NLON // LANES // 4

F32 = jnp.float32
BF16 = jnp.bfloat16
NT = (((1,), (1,)), ((), ()))


def dot(a, b, dims=(((1,), (0,)), ((), ()))):
    return lax.dot_general(a, b, dims, preferred_element_type=F32)


def iota(shape, dim):
    return lax.broadcasted_iota(jnp.int32, shape, dim)


def cos_sin(products, count, inverse, quarter=0):
    quarters = jnp.floor(products * 4.0 * inverse + 0.5)
    angle = (products * 4.0 - quarters * count) * inverse * (0.5 * math.pi)
    square = angle * angle
    sine = square * (1.0 / 362880.0) - 1.0 / 5040.0
    sine = square * sine + 1.0 / 120.0
    sine = square * sine - 1.0 / 6.0
    sine = angle + angle * (square * sine)
    cosine = square * (1.0 / 40320.0) - 1.0 / 720.0
    cosine = square * cosine + 1.0 / 24.0
    cosine = square * cosine - 0.5
    cosine = square * cosine + 1.0
    turn = (quarters.astype(jnp.int32) + quarter) & 3
    swap = (turn & 1) == 1
    first = jnp.where(swap, sine, cosine)
    second = jnp.where(swap, cosine, sine)
    first = jnp.where((turn == 1) | (turn == 2), -first, first)
    second = jnp.where(turn >= 2, -second, second)
    return first, second


def zonal_rows(sizes, count, sine, pair_ref, aux_ref):
    pairs, orders, parts, total_waves = sizes
    shape = (8, aux_ref.shape[1])
    sources = total_waves // 2 // pairs
    lane = iota(shape, 1)
    slot = (lane % sources) * pairs + (lane // (sources * orders)) % pairs
    number = jnp.zeros(shape, jnp.int32)
    for index in range(total_waves // 2):
        number = jnp.where(slot == index, pair_ref[index], number)
    second = (lane // sources) % orders == 1
    waves = jnp.where(second, total_waves - 1 - number, number).astype(F32)
    imag = lane // (shape[1] // parts)
    scale = 1.0 / (1.0 - jnp.full(shape, sine * sine)) / total_waves
    aux_ref[:8] = waves
    aux_ref[8:16] = jnp.where(imag == 1, -waves, waves) * scale
    aux_ref[16:] = jnp.full(shape, count)


def zonal_table(aux_ref, rows_ref, fine_ref, basis_ref):
    waves, count = aux_ref[:8], aux_ref[16:]
    shape = waves.shape
    lanes = shape[1]
    weight = jnp.where(waves == 0, 1.0, jnp.where(2 * waves < count, 2.0, 0.0))
    inverse = 1.0 / count
    index = iota(shape, 0)
    tile = (index // 2) * RUN + index % 2
    cosine, sine_part = cos_sin(waves * (tile * LANES).astype(F32), count, inverse)
    rows_ref[0], rows_ref[1] = cosine * weight, sine_part * weight
    rows_ref[2] = 2.0 * cosine
    groups = LANES // 8
    index = iota((groups, lanes), 0)
    cosine, sine_part = cos_sin(waves[:1] * (8 * index).astype(F32), count[:1], inverse[:1])
    rows_ref[3 : 3 + groups // 8] = cosine.reshape(groups // 8, 8, lanes)
    rows_ref[3 + groups // 8 :] = sine_part.reshape(groups // 8, 8, lanes)
    imag = iota(shape, 1) // (lanes // 2)
    lower_cos, lower_sin = cos_sin(waves * iota(shape, 0).astype(F32), count, inverse, imag)
    for g in range(groups):
        upper = pl.ds(g % 8, 1)
        c, s = rows_ref[3 + g // 8, upper], rows_ref[3 + groups // 8 + g // 8, upper]
        fine_ref[0, 8 * g : 8 * g + 8] = c * lower_cos - s * lower_sin
        fine_ref[1, 8 * g : 8 * g + 8] = -(s * lower_cos + c * lower_sin)
    def one(run, carry):
        zonal_run(run, rows_ref, fine_ref, basis_ref)
        return carry

    lax.fori_loop(0, NLON // LANES // RUN, one, 0)


def zonal_run(run, rows_ref, fine_ref, basis_ref):
    twice = rows_ref[2, 1:2]

    def first(t):
        a, b = rows_ref[0, pl.ds(2 * run + t, 1)], rows_ref[1, pl.ds(2 * run + t, 1)]
        return a * fine_ref[0] + b * fine_ref[1]

    def store(t, tile):
        start = pl.multiple_of((run * RUN + t) * LANES, LANES)
        basis_ref[pl.ds(start, LANES)] = tile.astype(BF16)

    before, here = first(0), first(1)
    store(0, before)
    store(1, here)
    for t in range(2, RUN):
        before, here = here, twice * here - before
        store(t, here)


def table_early():
    return 2 * lax.axis_index("wave") < lax.axis_size("wave")


def front_kernel(
    sizes,
    counts_hbm,
    sine_hbm,
    pair_hbm,
    legendre_hbm,
    slope_hbm,
    ops_hbm,
    spectral_hbm,
    send_ref,
    basis_ref,
    aux_ref,
    counts_ref,
    sine_ref,
    pair_ref,
    legendre_ref,
    slope_ref,
    ops_ref,
    spectral_ref,
    table_ref,
    main_ref,
    rest_ref,
    rows_ref,
    fine_ref,
    arrived,
):
    level_ranks, levels_out, total_waves = sizes
    pairs, fields, parts, width, levels = spectral_ref.shape
    _, orders, lats, full = legendre_ref.shape
    half = full // 2
    rank, row = lax.axis_index("lev"), lax.axis_index("wave")
    first_pair = row * pairs
    sub = pairs * orders
    rows = orders * lats
    copies = [
        pltpu.make_async_copy(source, target, arrived.at[index])
        for index, (source, target) in enumerate(
            [
                (counts_hbm, counts_ref),
                (sine_hbm, sine_ref),
                (pair_hbm, pair_ref),
                (legendre_hbm, legendre_ref),
                (slope_hbm, slope_ref),
                (ops_hbm, ops_ref),
            ]
            + [(spectral_hbm, spectral_ref)]
        )
    ]
    for copy in copies:
        copy.start()

    rest = levels_out - min(levels_out, MAIN)
    shape = (level_ranks * MAIN, levels)
    r, level = iota(shape, 0), iota(shape, 1)
    wanted = (r // MAIN) * levels_out + MAIN + r % REST
    chosen = (level == wanted) & (r % REST < rest)
    places = [(chosen & ((r % MAIN) // REST == g)).astype(F32).astype(BF16) for g in range(FIELDS)]

    for copy in copies[:3]:
        copy.wait()
    north = lax.rem(row, lats)
    sine = jnp.where(row < lats, sine_ref[north], -sine_ref[north])
    count = counts_ref[row].astype(F32)
    zonal = (pairs, orders, parts, total_waves)
    zonal_rows(zonal, count, sine, pair_ref, aux_ref)

    for copy in copies[3:5]:
        copy.wait()
    for t, ref in enumerate((legendre_ref, slope_ref)):
        for s in range(pairs):
            for w in range(orders):
                base = ((t * pairs + s) * orders + w) * lats
                table_ref[base : base + lats, :] = ref[s, w].astype(F32)
    table = table_ref[...]
    piece = table[:, :width]
    for b in range(1, level_ranks):
        piece = jnp.where(rank == b, table[:, b * width : (b + 1) * width], piece)
    shape = piece.shape
    r, position = iota(shape, 0), rank * width + iota(shape, 1)
    slot, order = (r // rows) % pairs, (r // lats) % orders
    number = jnp.zeros(shape, jnp.int32)
    for s in range(pairs):
        number = jnp.where(slot == s, pair_ref[first_pair + s], number)
    upper = (position >= half).astype(jnp.int32)
    offset = position - half * upper
    count0 = (total_waves - number + 1 - upper) >> 1
    count1 = (number + 2 - upper) >> 1
    low = jnp.where(order == 0, 0, count0)
    high = jnp.where(order == 0, count0, count0 + count1)
    piece = jnp.where((offset >= low) & (offset < high), piece, 0.0)
    plain = [piece[s * rows : (s + 1) * rows] for s in range(pairs)]
    slope = [piece[(pairs + s) * rows : (pairs + s + 1) * rows] for s in range(pairs)]
    both = [jnp.concatenate([a, b], axis=0).astype(BF16) for a, b in zip(plain, slope)]
    plain = [a.astype(BF16) for a in plain]

    for copy in copies[5:]:
        copy.wait()
    sums = [[] for _ in range(FIELDS)]
    for f in range(fields):
        for c in range(parts):
            for s in range(pairs):
                block = spectral_ref[s, f, c]
                if f == 2:
                    result = dot(both[s], block)
                    sums[3].append(result[rows:])
                    sums[2].append(result[:rows])
                else:
                    sums[f].append(dot(plain[s], block))

    operators = []
    for g, f in enumerate(FIELD_OF):
        below = LANES - levels - g * MAIN
        pieces = [ops_ref[f], jnp.zeros((below, levels), BF16)]
        if g:
            pieces = [jnp.zeros((g * MAIN, levels), BF16)] + pieces
        if rest:
            pieces.append(dot(places[g], ops_ref[f]).astype(BF16))
            pieces.append(jnp.zeros((LANES - level_ranks * MAIN, levels), BF16))
        operators.append(jnp.concatenate(pieces, axis=0))

    for g in range(FIELDS):
        exact = jnp.concatenate(sums[g], axis=0)
        high = exact.astype(BF16)
        low = (exact - high.astype(F32)).astype(BF16)
        both_terms = dot(jnp.concatenate([high, low], axis=0), operators[g], NT)
        sums[g] = both_terms[: exact.shape[0]] + both_terms[exact.shape[0] :]
    count_rows = pairs * rows
    lane = iota((parts * count_rows, LANES), 1)
    right = lane[:count_rows] >= LANES // parts
    south = jnp.where(rank * width < half, 1.0, -1.0)
    factor = jnp.where((iota((sub, LANES), 1) // MAIN) % FIELDS == FIELDS - 1, -south, south)
    for d in range(level_ranks):
        shift = d * levels_out
        joined = sums[0][:, :LANES]
        for g in range(1, FIELDS):
            joined = jnp.where(lane >= shift + g * MAIN, sums[g][:, :LANES], joined)
        real, imag = joined[:count_rows], joined[count_rows:]
        if shift:
            real = pltpu.roll(real, LANES - shift, 1)
        imag = pltpu.roll(imag, (LANES // parts - shift) % LANES, 1)
        main_ref[d] = jnp.where(right, imag, real)
        for j in range(lats):
            own = main_ref[d, pl.ds(j, sub, stride=lats), :]
            shape = (sub // 2, 2, LANES)
            for place, piece in ((j, own), (lats + j, own * factor)):
                send_ref[place * level_ranks + d, : sub // 2] = piece.astype(BF16).reshape(shape)
    if rest:
        block = MAIN
        total = (sums[0] + sums[1] + sums[2] + sums[3])[:, LANES:]
        total = total[:count_rows] + pltpu.roll(total[count_rows:], FIELDS * REST, 1)
        pieces = [total[s * rows : (s + 1) * rows] for s in range(pairs)]
        pieces = [pltpu.roll(x, s * block, 1) if s else x for s, x in enumerate(pieces)]
        lane = iota((rows, LANES), 1)
        lane_field = (iota((orders, LANES), 1) // REST) % FIELDS
        factor = jnp.where(lane_field == FIELDS - 1, -south, south)
        for d in range(level_ranks):
            joined = pieces[0]
            for s in range(1, pairs):
                joined = jnp.where(lane >= (d + s) * block, pieces[s], joined)
            if d:
                joined = pltpu.roll(joined, LANES - d * block, 1)
            rest_ref[d] = joined
            for j in range(lats):
                own = rest_ref[d, pl.ds(j, orders, stride=lats), :]
                for place, piece in ((j, own), (lats + j, own * factor)):
                    send_ref[place * level_ranks + d, sub // 2] = piece.astype(BF16)

    @pl.when(table_early())
    def _():
        zonal_table(aux_ref, rows_ref, fine_ref, basis_ref)


def grid_kernel(
    sizes,
    received_ref,
    early_ref,
    aux_ref,
    out_hbm,
    out_ref,
    main_ref,
    rest_ref,
    rows_ref,
    fine_ref,
    late_ref,
    sent,
):
    refs = (out_hbm, out_ref, main_ref, rest_ref, sent)
    early = table_early()

    @pl.when(early)
    def _():
        grid_step(sizes, received_ref, early_ref, aux_ref, *refs)

    @pl.when(jnp.logical_not(early))
    def _():
        zonal_table(aux_ref, rows_ref, fine_ref, late_ref)
        grid_step(sizes, received_ref, late_ref, aux_ref, *refs)


def grid_step(
    sizes, received_ref, basis_ref, aux_ref, out_hbm, out_ref, main_ref, rest_ref, sent
):
    level_ranks, levels_out, pairs, orders, total_waves = sizes
    sub = pairs * orders
    main_levels = min(levels_out, MAIN)
    rest = levels_out - main_levels

    sources = received_ref.shape[0] // level_ranks
    half = sub * sources
    derivative = aux_ref[8:9]
    scale = -1.0 / total_waves
    if rest:
        for a in range(sources):
            parts = [received_ref[a * level_ranks + b, sub // 2] for b in range(level_ranks)]
            rest_ref[orders * a : orders * (a + 1)] = sum(x.astype(F32) for x in parts)
        stacked = [rest_ref[pl.ds(w, sources, stride=orders), :] for w in range(orders)]
        turned = jnp.concatenate(stacked, axis=0).T
        block = FIELDS * REST
        pieces = [
            turned[s * MAIN + c * block : s * MAIN + (c + 1) * block]
            for c in range(2)
            for s in range(pairs)
        ]
        extra = jnp.concatenate(pieces, axis=1)
        field = iota(extra.shape, 0) // REST
        swapped = pltpu.roll(extra, half, 1) * derivative
        extra = jnp.where(field == 2, swapped, jnp.where(field == 1, extra * scale, extra))
    for a in range(sources):
        parts = [received_ref[a * level_ranks + b, : sub // 2] for b in range(level_ranks)]
        main_ref[sub * a : sub * (a + 1)] = sum(x.astype(F32) for x in parts).reshape(sub, LANES)
    stacked = [main_ref[pl.ds(i, sources, stride=sub), :] for i in range(sub)]
    turned = jnp.concatenate(stacked, axis=0).T
    coeffs = jnp.concatenate([turned[: LANES // 2], turned[LANES // 2 :]], axis=1)
    coeffs = [coeffs[g * MAIN : (g + 1) * MAIN] for g in range(FIELDS)]
    coeffs[2] = pltpu.roll(coeffs[2], half, 1) * derivative
    coeffs[1] = coeffs[1] * scale
    coeffs = jnp.concatenate(coeffs + ([extra] if rest else []), axis=0).astype(BF16)

    count = aux_ref[16:17, :1].astype(jnp.int32)
    copies = []
    start = 0
    for index, size in enumerate(COLUMNS):
        values = dot(coeffs, basis_ref[start : start + size], NT)
        inside = start + iota((1, size), 1) < count
        first, second, third, slope = (values[g * MAIN : (g + 1) * MAIN] for g in range(FIELDS))
        result = jnp.where(inside, first * third + second * slope, 0.0)
        out_ref[:main_levels, 0, start : start + size] = result[:main_levels]
        if rest:
            value = values[FIELDS * MAIN :]
            product = value * pltpu.roll(value, 2 * REST, 0)
            result = product[:REST] + product[REST : 2 * REST]
            result = jnp.where(inside, result, 0.0)
            out_ref[main_levels:, 0, start : start + size] = result[:rest]
        window = (slice(None), slice(None), slice(start, start + size))
        copy = pltpu.make_async_copy(out_ref.at[window], out_hbm.at[window], sent.at[index])
        copy.start()
        copies.append(copy)
        start += size
    for copy in copies:
        copy.wait()


def per_device(spectral, vertical_ops, legendre, legendre_slope, sine_lat, pair_map, lon_counts):
    pairs, fields, parts, levels, width = spectral.shape
    level_ranks = lax.axis_size("lev")
    rows = lax.axis_size("wave")
    slots = pair_map.shape[0]
    total_waves = 2 * slots
    levels_out = levels // level_ranks
    lats, full = legendre.shape[2:]
    orders = legendre.shape[1]
    group = pairs * orders
    assert rows == 2 * lats == lon_counts.shape[0]
    rest = max(levels_out - MAIN, 0)
    assert rest <= REST and levels + FIELDS * MAIN - MAIN <= LANES
    assert parts * FIELDS * MAIN == LANES and group % 2 == 0
    assert not rest or level_ranks + pairs - 1 <= LANES // MAIN
    assert (full // 2) % width == 0

    vmem = pl.BlockSpec(memory_space=pltpu.VMEM)
    hbm = pl.BlockSpec(memory_space=pl.ANY)
    by_position = jnp.transpose(spectral, (0, 1, 2, 4, 3))
    resident = 4 * slots * NLON * 2 <= RESIDENT
    placed = pltpu.VMEM if resident else jax.ShapeDtypeStruct
    sources = [lon_counts, sine_lat, pair_map]
    sources += [legendre, legendre_slope, vertical_ops, by_position]
    tables = [
        pltpu.VMEM((3 + LANES // 32, 8, 2 * parts * slots), F32),
        pltpu.VMEM((2, LANES, 2 * parts * slots), F32),
    ]
    spaces = [pltpu.SMEM] * 3 + [pltpu.VMEM] * 4
    send, basis, aux = pl.pallas_call(
        functools.partial(front_kernel, (level_ranks, levels_out, total_waves)),
        out_shape=[
            pltpu.VMEM((rows * level_ranks, group // 2 + (rest > 0), 2, LANES), BF16),
            placed((NLON, 2 * parts * slots), BF16),
            pltpu.VMEM((24, 2 * parts * slots), F32),
        ],
        in_specs=[hbm] * len(sources),
        out_specs=[vmem] * 3,
        scratch_shapes=[space(x.shape, x.dtype) for space, x in zip(spaces, sources)]
        + [
            pltpu.VMEM((2 * group * lats, full), F32),
            pltpu.VMEM((level_ranks, group * lats, LANES), F32),
            pltpu.VMEM((level_ranks, orders * lats, LANES), F32),
            *tables,
            pltpu.SemaphoreType.DMA((len(sources),)),
        ],
        name="front",
    )(*sources)
    received = lax.all_to_all(send, ("wave", "lev"), split_axis=0, concat_axis=0, tiled=True)
    received, aux = (
        pltpu.with_memory_space_constraint(x, pltpu.VMEM) for x in (received, aux)
    )
    if resident:
        basis = pltpu.with_memory_space_constraint(basis, pltpu.VMEM)
    return pl.pallas_call(
        functools.partial(grid_kernel, (level_ranks, levels_out, pairs, orders, total_waves)),
        out_shape=jax.ShapeDtypeStruct((levels_out, 1, NLON), F32),
        in_specs=[vmem, vmem, vmem],
        out_specs=hbm,
        scratch_shapes=[
            pltpu.VMEM((levels_out, 1, NLON), F32),
            pltpu.VMEM((rows * group, LANES), F32),
            pltpu.VMEM((rows * orders, LANES), F32),
            *tables,
            pltpu.VMEM((NLON, 2 * parts * slots), BF16),
            pltpu.SemaphoreType.DMA((len(COLUMNS),)),
        ],
        name="grid_tendency",
    )(received, basis, aux)


def solution(mesh):
    placed = (
        P("wave", None, None, None, "lev"),
        P(),
        P("wave", None, None, None),
        P("wave", None, None, None),
        P(),
        P(),
        P(),
    )
    return jax.shard_map(
        per_device, mesh=mesh, in_specs=placed, out_specs=P("lev", "wave", None), check_vma=False
    )
```
